256 devices in a mesh: row: 8 (over x, core), col: 32 (over z, y).
Axes of the slice: x: 4, y: 4, z: 8, core: 2. Of those that a mesh axis runs over, the one named last changes fastest.
Arguments:
- density: bfloat16 [256, 16, 128, 128], P(('row', 'col')), as said below
- cols: int32 [256, 16], replicated, may hold values from 0 to 255, as said below
Outputs:
- new_density: float32 [256, 16, 128, 128], P(('row', 'col'))
The draws below stay inside these ranges and needn't reach their ends.
Inputs may be any that keep to these rules, and one draw needn't show every extreme that they name: Block row b is held by the device with row index (b) // 32 and col index q = (b) % 32. cols[b, 0] = b and a row's entries are distinct. For 1 <= t <= 7, cols[b, 2t - 1] is held by a device of col index q + t and cols[b, 2t] by one of col index q - t (modulo 32); cols[b, 15] by one of col index q + 16. The pattern is symmetric with mirrored slots: if j = cols[b, s] then cols[j, s'] = b, where s' = s for s = 0 and s = 15, s' = s + 1 for odd s below 15, and s' = s - 1 for even s above 0. density[b, s] is exactly the transpose of density[cols[b, s], s'], with s' the mirrored slot.
All inputs are finite; a program needn't handle non-finite values.
Results may differ from the reference program's by a relative error of at most 0.0093.
Values may be sent and summed in bfloat16 or wider, within the bound.
No kernel may reach another device: no remote copies, remote signals or barrier semaphores. Data moves between devices by JAX's collectives and lax.ppermute only.
A program may use at most 128 MiB of HBM per device.

```python
import math
import jax
import jax.numpy as jnp
import numpy as np
from jax import lax

BS = 128
RD = 1
NZ = 16
NB = 256
N_ROW = 8
N_COL = 32


def block_pattern(key):
    half_count = (NZ - 2) // 2
    column_size = N_ROW * RD
    key_list = jax.random.split(key, half_count * N_COL + N_COL)
    shuffles = jax.vmap(lambda single: jax.random.permutation(single, column_size))(key_list)
    columns = jnp.arange(N_COL, dtype=jnp.int32)
    ranks = jnp.arange(column_size, dtype=jnp.int32)

    def global_index(rank_grid, col_grid):
        return (rank_grid // RD * N_COL + col_grid) * RD + rank_grid % RD
    slot_list = [global_index(jnp.broadcast_to(ranks[:, None], (column_size, N_COL)), jnp.broadcast_to(columns[None, :], (column_size, N_COL)))]
    for stride in range(1, half_count + 1):
        upward = shuffles[(stride - 1) * N_COL:stride * N_COL]
        downward = jnp.argsort(upward, axis=1).astype(jnp.int32)
        up_cols = (columns + stride) % N_COL
        down_cols = (columns - stride) % N_COL
        slot_list.append(global_index(upward.T, jnp.broadcast_to(up_cols[None, :], (column_size, N_COL))))
        slot_list.append(global_index(downward[down_cols].T, jnp.broadcast_to(down_cols[None, :], (column_size, N_COL))))
    opposite = shuffles[half_count * N_COL:]
    opposite_back = jnp.argsort(opposite, axis=1).astype(jnp.int32)
    middle = N_COL // 2
    lower_half = columns < middle
    partner_rank = jnp.where(lower_half[None, :], opposite.T, opposite_back[(columns - middle) % N_COL].T)
    far_cols = (columns + middle) % N_COL
    slot_list.append(global_index(partner_rank, jnp.broadcast_to(far_cols[None, :], (column_size, N_COL))))
    pattern = jnp.stack(slot_list, axis=-1)
    pattern = pattern.reshape(N_ROW, RD, N_COL, NZ).transpose(0, 2, 1, 3).reshape(NB, NZ)
    return pattern.astype(jnp.int32)


def mirror_table():
    order = [0]
    for stride in range(1, (NZ - 2) // 2 + 1):
        order = order + [2 * stride, 2 * stride - 1]
    return np.array(order + [NZ - 1], dtype=np.int32)


def draw_cols(key, part):
    return block_pattern(jax.random.fold_in(key, 11))


def draw_density(key, part):
    pattern = block_pattern(jax.random.fold_in(key, 11))
    noise_key, level_key = jax.random.split(jax.random.fold_in(key, 12))
    spread = 0.7 * math.sqrt(2.0) / math.sqrt(BS * NZ)
    noise = jax.random.normal(noise_key, (NB, NZ, BS, BS), jnp.float32) * spread
    levels = jax.random.uniform(level_key, (NB, BS), jnp.float32, 0.05, 0.95)
    mirror = jnp.array(mirror_table())
    partner = noise[pattern, mirror[None, :]]
    symmetric = 0.5 * (noise + jnp.swapaxes(partner, -1, -2))
    diagonal = levels[:, :, None] * jnp.eye(BS, dtype=jnp.float32)[None, :, :]
    symmetric = symmetric.at[:, 0].add(diagonal)
    return symmetric.astype(jnp.bfloat16)


def setup_inputs(seed: int = 0) -> dict:
    arg_keys = jax.random.split(jax.random.key(seed), 3)
    density = draw_density(jax.random.fold_in(arg_keys[2], 71), 0)
    cols = draw_cols(jax.random.fold_in(arg_keys[2], 71), 0)
    return dict(density=density, cols=cols)


def locate(lists, targets, slot_ids):
    matches = lists == targets[..., None]
    found = jnp.sum(jnp.where(matches, slot_ids, 0), axis=-1).astype(jnp.int32)
    return found, jnp.any(matches, axis=-1)


def reference(density, cols):
    slot_count = cols.shape[1]
    slot_ids = jnp.arange(slot_count, dtype=jnp.int32)
    blocks = density.astype(jnp.float32)
    inner_lists = cols[cols]

    def product(operand):
        results = []
        for column_slot in range(slot_count):
            target = cols[:, column_slot]
            found, present = locate(inner_lists, target[:, None], slot_ids)
            picked = operand[cols, found]
            picked = jnp.where(present[..., None, None], picked, jnp.zeros((), picked.dtype))
            results.append(jnp.einsum("itab,itbc->iac", blocks, picked, precision=lax.Precision.HIGHEST))
        return jnp.stack(results, axis=1)

    square = product(blocks)
    square_half = lax.optimization_barrier(square.astype(jnp.bfloat16))
    cube = product(square_half.astype(jnp.float32))
    return 3.0 * square - 2.0 * cube
```

```python
import functools

import jax
import jax.numpy as jnp
from jax import lax
from jax.experimental import pallas as pl
from jax.experimental.pallas import tpu as pltpu
from jax.sharding import PartitionSpec as P

SIGNS = {1: 1, 2: 1, 3: -1, 4: 1, 5: 1, 6: -1, 7: -1}


class Plan:
    def __init__(self, slot_count, grid_cols, grid_rows):
        half = (slot_count - 2) // 2
        self.slot_count, self.grid_cols, self.grid_rows = slot_count, grid_cols, grid_rows
        self.far = grid_cols // 2
        self.offsets = [0]
        for stride in range(1, half + 1):
            self.offsets += [stride, -stride]
        self.offsets.append(self.far)
        self.slot = {o: s for s, o in enumerate(self.offsets)}
        self.tiles = [0] + [SIGNS.get(d, 1) * d for d in range(1, half + 1)] + [self.far]
        self.tile = {d: t for t, d in enumerate(self.tiles)}
        near = [o for o in self.offsets if o not in (0, self.far)]
        self.left = {self.far: []}
        for d in self.tiles[1:-1]:
            self.left[d] = [a for a in near if a != d and self.near(a - d)]
        self.edges = {self.far: []}
        for a in near:
            self.edges[a] = [b for b in near if b != a and (a - b) in self.tile]
        self.moved = [o for o in self.offsets if o != 0]

    def near(self, o):
        return o in self.slot and o != self.far

    def row_id(self, rank, col):
        return rank * self.grid_cols + lax.rem(col + 2 * self.grid_cols, self.grid_cols)


def shifted(value, by):
    length = lax.axis_size("col")
    return lax.ppermute(value, "col", [(i, (i + by) % length) for i in range(length)])


def nn(a, b):
    return lax.dot_general(a, b, (((1,), (0,)), ((), ())), preferred_element_type=jnp.float32)


def nt(a, b):
    return lax.dot_general(a, b, (((1,), (1,)), ((), ())), preferred_element_type=jnp.float32)


def tn(a, b):
    return lax.dot_general(a, b, (((0,), (0,)), ((), ())), preferred_element_type=jnp.float32)


def gather_rows(block):
    length = lax.axis_size("row")
    chips = length // 2
    pieces = []
    for step in range(chips):
        if step == 0:
            same = block
        else:
            same = lax.ppermute(
                block, "row",
                [(2 * x + h, 2 * ((x + step) % chips) + h) for x in range(chips) for h in range(2)],
            )
        pieces.append(same)
    out = []
    for same in pieces:
        out += [same, lax.ppermute(same, "row", [(i, i ^ 1) for i in range(length)])]
    return out


def piece_rank(plan, my_row, index):
    chips = plan.grid_rows // 2
    x = lax.rem(my_row // 2 - index // 2 + chips, chips)
    core = lax.rem(my_row, 2)
    if index % 2:
        core = 1 - core
    return 2 * x + core


def land(plan, my_row, pieces, panel, sems):
    copies = []
    for index, piece in enumerate(pieces):
        copy = pltpu.make_async_copy(piece, panel.at[piece_rank(plan, my_row, index)], sems.at[index])
        copy.start()
        copies.append(copy)
    return copies


def square_kernel(plan, *refs):
    cols, own = refs[0], refs[1]
    n_left = len(plan.tiles) - 1
    lefts = dict(zip(plan.tiles[1:], refs[2:2 + n_left]))
    pieces = refs[2 + n_left:2 + n_left + plan.grid_rows]
    out, self_square, panel, total, sems = refs[2 + n_left + plan.grid_rows:]
    n = plan.slot_count
    my_row, my_col = lax.axis_index("row"), lax.axis_index("col")
    copies = land(plan, my_row, pieces, panel, sems)
    acc = nt(own[0], own[0])
    for s in range(1, n):
        acc = acc + nt(own[s], own[s])
    self_square[...] = acc
    out[0] = acc.astype(out.dtype)
    for copy in copies:
        copy.wait()
    for t, d in enumerate(plan.tiles):
        if d == 0:
            continue
        left = lefts[d]
        i = plan.row_id(my_row, my_col - d)
        j = cols[i * n + plan.slot[d]]
        rank = j // plan.grid_cols
        back = plan.slot[-d] if d != plan.far else plan.slot[d]
        total[...] = nt(left[0], panel[rank, back]) + tn(panel[rank, back], panel[rank, 0])
        for p, a in enumerate(plan.left[d]):
            k = cols[i * n + plan.slot[a]]
            u = plan.slot[a - d]

            @pl.when(cols[j * n + u] == k)
            def _():
                total[...] += nt(left[p + 1], panel[rank, u])

        out[t] = total[...].astype(out.dtype)


def pick_kernel(plan, *refs):
    cols, own = refs[0], refs[1]
    pieces = refs[2:2 + plan.grid_rows]
    rest = refs[2 + plan.grid_rows:]
    n_out = len(plan.moved) + 1
    outs, (panel, sems) = rest[:n_out], rest[n_out:]
    n = plan.slot_count
    my_row, my_col = lax.axis_index("row"), lax.axis_index("col")
    copies = land(plan, my_row, pieces, panel, sems)
    for copy in copies:
        copy.wait()
    for out, a in zip(outs, plan.moved):
        i = plan.row_id(my_row, my_col - a)
        k = cols[i * n + plan.slot[a]]
        out[0] = panel[k // plan.grid_cols, 0]
        p = 1
        if a in plan.tile and a != plan.far:
            out[p] = own[plan.tile[a]]
            p += 1
        for b in plan.edges[a]:
            j = cols[i * n + plan.slot[b]]
            out[p] = panel[j // plan.grid_cols, plan.tile[a - b]]
            p += 1
    i = plan.row_id(my_row, my_col)
    for p, d in enumerate(plan.tiles[1:]):
        back = plan.slot[-d] if d != plan.far else plan.slot[d]
        j = cols[i * n + back]
        outs[-1][p] = panel[j // plan.grid_cols, plan.tile[d]]


def message_size(plan, a):
    return 1 + (1 if a in plan.tile and a != plan.far else 0) + len(plan.edges[a])


def cube_kernel(plan, *refs):
    cols, own, self_square, local = refs[:4]
    arrived = dict(zip(plan.moved, refs[4:4 + len(plan.moved)]))
    out = refs[4 + len(plan.moved)]
    n = plan.slot_count
    my_row, my_col = lax.axis_index("row"), lax.axis_index("col")
    i = plan.row_id(my_row, my_col)
    s_self = self_square[...]
    acc = nn(own[0], s_self.astype(own.dtype))
    for a in plan.moved:
        t = plan.slot[a]
        diagonal = arrived[a][0]
        if a in plan.tile and a != plan.far:
            s_ia = arrived[a][1]
            acc = acc + nt(own[t], s_ia)
            cube = nn(own[0], s_ia) + nn(own[t], diagonal)
            mine = s_ia.astype(jnp.float32)
        else:
            s_ai = local[plan.tile[-a if a != plan.far else a] - 1]
            acc = acc + nn(own[t], s_ai)
            cube = nt(own[0], s_ai) + nn(own[t], diagonal)
            mine = s_ai.astype(jnp.float32).T
        out[0, t] = 3.0 * mine - 2.0 * cube
    out[0, 0] = 3.0 * s_self - 2.0 * acc
    for a in plan.moved:
        p = 2 if a in plan.tile and a != plan.far else 1
        for b in plan.edges[a]:
            k, j = cols[i * n + plan.slot[a]], cols[i * n + plan.slot[b]]

            @pl.when(cols[j * n + plan.slot[a - b]] == k)
            def _():
                edge = arrived[a][p]
                ta, tb = plan.slot[a], plan.slot[b]
                out[0, tb] += -2.0 * nt(own[ta], edge)
                out[0, ta] += -2.0 * nn(own[tb], edge)

            p += 1


VMEM = pl.BlockSpec(memory_space=pltpu.VMEM)
SMEM = pl.BlockSpec(memory_space=pltpu.SMEM)
ANY = pl.BlockSpec(memory_space=pl.ANY)
PARAMS = pltpu.CompilerParams(vmem_limit_bytes=48 << 20)


def per_device(density, cols):
    slot_count, size = density.shape[1], density.shape[2]
    plan = Plan(slot_count, lax.axis_size("col"), lax.axis_size("row"))
    own = density[0]
    table = cols.reshape(-1)
    block = (size, size)
    n_tiles = len(plan.tiles)
    lefts = []
    for d in plan.tiles[1:]:
        slots = [0] + [plan.slot[a] for a in plan.left[d]]
        message = jnp.concatenate([own[s:s + 1] for s in slots], axis=0)
        lefts.append(shifted(message, d))
    panel = gather_rows(own)
    rows = plan.grid_rows
    tiles, self_square = pl.pallas_call(
        functools.partial(square_kernel, plan),
        out_shape=[
            jax.ShapeDtypeStruct((n_tiles, *block), own.dtype),
            jax.ShapeDtypeStruct(block, jnp.float32),
        ],
        in_specs=[SMEM, VMEM] + [VMEM] * len(lefts) + [ANY] * rows,
        out_specs=[VMEM, VMEM],
        scratch_shapes=[
            pltpu.VMEM((rows, slot_count, *block), own.dtype),
            pltpu.VMEM(block, jnp.float32),
            pltpu.SemaphoreType.DMA((rows,)),
        ],
        compiler_params=PARAMS,
        name="square",
    )(table, own, *lefts, *panel)
    square_panel = gather_rows(tiles)
    picked = pl.pallas_call(
        functools.partial(pick_kernel, plan),
        out_shape=[
            jax.ShapeDtypeStruct((message_size(plan, a), *block), own.dtype) for a in plan.moved
        ] + [jax.ShapeDtypeStruct((n_tiles - 1, *block), own.dtype)],
        in_specs=[SMEM, VMEM] + [ANY] * rows,
        out_specs=[VMEM] * (len(plan.moved) + 1),
        scratch_shapes=[
            pltpu.VMEM((rows, n_tiles, *block), own.dtype),
            pltpu.SemaphoreType.DMA((rows,)),
        ],
        compiler_params=PARAMS,
        name="pick",
    )(table, tiles, *square_panel)
    arrived = [shifted(m, -a) for m, a in zip(picked, plan.moved)]
    return pl.pallas_call(
        functools.partial(cube_kernel, plan),
        out_shape=jax.ShapeDtypeStruct((1, slot_count, *block), jnp.float32),
        in_specs=[SMEM, VMEM, VMEM, VMEM] + [VMEM] * len(arrived),
        out_specs=VMEM,
        compiler_params=PARAMS,
        name="cube",
    )(table, own, self_square, picked[-1], *arrived)


def solution(mesh):
    in_specs = (P(("row", "col"), None, None, None), P())
    out_specs = P(("row", "col"), None, None, None)
    return jax.shard_map(
        per_device, mesh=mesh, in_specs=in_specs, out_specs=out_specs, check_vma=False
    )
```

```python
import functools

import jax
import jax.numpy as jnp
from jax import lax
from jax.experimental import pallas as pl
from jax.experimental.pallas import tpu as pltpu
from jax.sharding import PartitionSpec as P

SIGNS = {1: 1, 2: -1, 3: 1, 4: 1, 5: -1, 6: 1, 7: -1}
LEFT_ORDER = [-7, -5, 4, 3, 1, -2, 16, 6]
BACK_ORDER = [5, 6, -7, -1, -5, -3, 4, -2, 7, -4, 3, 1, 2, 16, -6]
LEFT_WINDOW = 4
BACK_WINDOW = 4


class Plan:
    def __init__(self, slot_count, grid_cols, grid_rows):
        half = (slot_count - 2) // 2
        self.slot_count, self.grid_cols, self.grid_rows = slot_count, grid_cols, grid_rows
        self.far = grid_cols // 2
        self.offsets = [0]
        for stride in range(1, half + 1):
            self.offsets += [stride, -stride]
        self.offsets.append(self.far)
        self.slot = {o: s for s, o in enumerate(self.offsets)}
        self.tiles = [0] + [SIGNS.get(d, 1) * d for d in range(1, half + 1)] + [self.far]
        self.tile = {d: t for t, d in enumerate(self.tiles)}
        near = [o for o in self.offsets if o not in (0, self.far)]
        self.left = {self.far: []}
        for d in self.tiles[1:-1]:
            self.left[d] = [a for a in near if a != d and self.near(a - d)]
        self.edges = {self.far: []}
        for a in near:
            self.edges[a] = [b for b in near if b != a and (a - b) in self.tile]
        self.moved = [o for o in self.offsets if o != 0]

    def near(self, o):
        return o in self.slot and o != self.far

    def row_id(self, rank, col):
        return rank * self.grid_cols + lax.rem(col + 2 * self.grid_cols, self.grid_cols)


def shifted(value, by):
    length = lax.axis_size("col")
    return lax.ppermute(value, "col", [(i, (i + by) % length) for i in range(length)])


def in_turn(values, sends, order, window):
    results, last = {}, []
    for key in order:
        value = values[key]
        if len(last) >= window:
            value, _ = lax.optimization_barrier((value, last[-window]))
        results[key] = sends[key](value)
        last.append(results[key])
    return results


def ordered(preferred, keys):
    return [k for k in preferred if k in keys] + [k for k in keys if k not in preferred]


def nn(a, b):
    return lax.dot_general(a, b, (((1,), (0,)), ((), ())), preferred_element_type=jnp.float32)


def nt(a, b):
    return lax.dot_general(a, b, (((1,), (1,)), ((), ())), preferred_element_type=jnp.float32)


def tn(a, b):
    return lax.dot_general(a, b, (((0,), (0,)), ((), ())), preferred_element_type=jnp.float32)


def gather_rows(block):
    length = lax.axis_size("row")
    chips = length // 2
    pieces = []
    for step in range(chips):
        if step == 0:
            same = block
        else:
            same = lax.ppermute(
                block, "row",
                [(2 * x + h, 2 * ((x + step) % chips) + h) for x in range(chips) for h in range(2)],
            )
        pieces.append(same)
    out = []
    for same in pieces:
        out += [same, lax.ppermute(same, "row", [(i, i ^ 1) for i in range(length)])]
    return out


def piece_rank(plan, my_row, index):
    chips = plan.grid_rows // 2
    x = lax.rem(my_row // 2 - index // 2 + chips, chips)
    core = lax.rem(my_row, 2)
    if index % 2:
        core = 1 - core
    return 2 * x + core


def land(plan, my_row, pieces, panel, sems):
    copies = []
    for index, piece in enumerate(pieces):
        copy = pltpu.make_async_copy(piece, panel.at[piece_rank(plan, my_row, index)], sems.at[index])
        copy.start()
        copies.append(copy)
    return copies


def pack_kernel(plan, own, *outs):
    for out, d in zip(outs, plan.tiles[1:]):
        for p, s in enumerate([0] + [plan.slot[a] for a in plan.left[d]]):
            out[p] = own[s]


def square_kernel(plan, *refs):
    cols, own = refs[0], refs[1]
    n_left = len(plan.tiles) - 1
    pieces = refs[2 + n_left:2 + n_left + plan.grid_rows]
    rest = refs[2 + n_left + plan.grid_rows:]
    out, far_out, self_square, panel, total, sems, left_sems = rest[:7]
    lefts = dict(zip(plan.tiles[1:], rest[7:]))
    n = plan.slot_count
    my_row, my_col = lax.axis_index("row"), lax.axis_index("col")
    copies = land(plan, my_row, pieces, panel, sems)
    for t in range(n_left):
        copy = pltpu.make_async_copy(refs[2 + t], rest[7 + t], left_sems.at[t])
        copy.start()
        copies.append(copy)
    acc = nt(own[0], own[0])
    for s in range(1, n):
        acc = acc + nt(own[s], own[s])
    self_square[...] = acc
    out[0] = acc.astype(out.dtype)
    for copy in copies:
        copy.wait()
    for t, d in enumerate(plan.tiles):
        if d == 0:
            continue
        left = lefts[d]
        i = plan.row_id(my_row, my_col - d)
        j = cols[i * n + plan.slot[d]]
        rank = j // plan.grid_cols
        back = plan.slot[-d] if d != plan.far else plan.slot[d]
        total[...] = nt(left[0], panel[rank, back]) + tn(panel[rank, back], panel[rank, 0])
        for p, a in enumerate(plan.left[d]):
            k = cols[i * n + plan.slot[a]]
            u = plan.slot[a - d]

            @pl.when(cols[j * n + u] == k)
            def _():
                total[...] += nt(left[p + 1], panel[rank, u])

        if d == plan.far:
            far_out[0] = total[...].astype(out.dtype)
        else:
            out[t] = total[...].astype(out.dtype)


def pick_kernel(plan, *refs):
    cols, own, far = refs[0], refs[1], refs[2]
    pieces = refs[3:3 + plan.grid_rows]
    rest = refs[3 + plan.grid_rows:]
    n_out = len(plan.moved) + 1
    outs, (panel, sems) = rest[:n_out], rest[n_out:]
    n = plan.slot_count
    my_row, my_col = lax.axis_index("row"), lax.axis_index("col")
    copies = land(plan, my_row, pieces, panel, sems)
    for copy in copies:
        copy.wait()
    for out, a in zip(outs, plan.moved):
        i = plan.row_id(my_row, my_col - a)
        k = cols[i * n + plan.slot[a]]
        out[0] = panel[k // plan.grid_cols, 0]
        p = 1
        if a == plan.far:
            out[p] = far[0]
        elif a in plan.tile:
            out[p] = own[plan.tile[a]]
            p += 1
        for b in plan.edges[a]:
            j = cols[i * n + plan.slot[b]]
            out[p] = panel[j // plan.grid_cols, plan.tile[a - b]]
            p += 1
    i = plan.row_id(my_row, my_col)
    for p, d in enumerate(plan.tiles[1:-1]):
        j = cols[i * n + plan.slot[-d]]
        outs[-1][p] = panel[j // plan.grid_cols, plan.tile[d]]


def message_size(plan, a):
    return 1 + (1 if a in plan.tile else 0) + len(plan.edges[a])


def cube_kernel(plan, *refs):
    cols, own, self_square, local = refs[:4]
    arrived = dict(zip(plan.moved, refs[4:4 + len(plan.moved)]))
    out = refs[4 + len(plan.moved)]
    n = plan.slot_count
    my_row, my_col = lax.axis_index("row"), lax.axis_index("col")
    i = plan.row_id(my_row, my_col)
    s_self = self_square[...]
    acc = nn(own[0], s_self.astype(own.dtype))
    for a in plan.moved:
        t = plan.slot[a]
        diagonal = arrived[a][0]
        if a in plan.tile:
            s_ia = arrived[a][1]
            acc = acc + nt(own[t], s_ia)
            cube = nn(own[0], s_ia) + nn(own[t], diagonal)
            mine = s_ia.astype(jnp.float32)
        else:
            s_ai = local[plan.tile[-a] - 1]
            acc = acc + nn(own[t], s_ai)
            cube = nt(own[0], s_ai) + nn(own[t], diagonal)
            mine = s_ai.astype(jnp.float32).T
        out[0, t] = 3.0 * mine - 2.0 * cube
    out[0, 0] = 3.0 * s_self - 2.0 * acc
    for a in plan.moved:
        p = 2 if a in plan.tile else 1
        for b in plan.edges[a]:
            k, j = cols[i * n + plan.slot[a]], cols[i * n + plan.slot[b]]

            @pl.when(cols[j * n + plan.slot[a - b]] == k)
            def _():
                edge = arrived[a][p]
                ta, tb = plan.slot[a], plan.slot[b]
                out[0, tb] += -2.0 * nt(own[ta], edge)
                out[0, ta] += -2.0 * nn(own[tb], edge)

            p += 1


VMEM = pl.BlockSpec(memory_space=pltpu.VMEM)
SMEM = pl.BlockSpec(memory_space=pltpu.SMEM)
ANY = pl.BlockSpec(memory_space=pl.ANY)
SMALL = pltpu.CompilerParams(vmem_limit_bytes=24 << 20)


def per_device(density, cols):
    slot_count, size = density.shape[1], density.shape[2]
    plan = Plan(slot_count, lax.axis_size("col"), lax.axis_size("row"))
    own = density[0]
    table = cols.reshape(-1)
    block = (size, size)
    rows, tiles = plan.grid_rows, plan.tiles
    sizes = {d: 1 + len(plan.left[d]) for d in tiles[1:]}
    panel = gather_rows(own)
    packed = pl.pallas_call(
        functools.partial(pack_kernel, plan),
        out_shape=[jax.ShapeDtypeStruct((sizes[d], *block), own.dtype) for d in tiles[1:]],
        in_specs=[VMEM],
        out_specs=[VMEM] * len(sizes),
        compiler_params=SMALL,
        name="pack",
    )(own)
    sends = {d: functools.partial(shifted, by=d) for d in tiles[1:]}
    lefts = in_turn(
        dict(zip(tiles[1:], packed)), sends, ordered(LEFT_ORDER, tiles[1:]), LEFT_WINDOW
    )
    squares, far_square, self_square = pl.pallas_call(
        functools.partial(square_kernel, plan),
        out_shape=[
            jax.ShapeDtypeStruct((len(tiles) - 1, *block), own.dtype),
            jax.ShapeDtypeStruct((1, *block), own.dtype),
            jax.ShapeDtypeStruct(block, jnp.float32),
        ],
        in_specs=[SMEM, VMEM] + [ANY] * len(lefts) + [ANY] * rows,
        out_specs=[VMEM, VMEM, VMEM],
        scratch_shapes=[
            pltpu.VMEM((rows, slot_count, *block), own.dtype),
            pltpu.VMEM(block, jnp.float32),
            pltpu.SemaphoreType.DMA((rows,)),
            pltpu.SemaphoreType.DMA((len(lefts),)),
        ] + [pltpu.VMEM((sizes[d], *block), own.dtype) for d in tiles[1:]],
        compiler_params=SMALL,
        name="square",
    )(table, own, *[lefts[d] for d in tiles[1:]], *panel)
    square_panel = gather_rows(squares)
    picked = pl.pallas_call(
        functools.partial(pick_kernel, plan),
        out_shape=[
            jax.ShapeDtypeStruct((message_size(plan, a), *block), own.dtype) for a in plan.moved
        ] + [jax.ShapeDtypeStruct((len(tiles) - 2, *block), own.dtype)],
        in_specs=[SMEM, VMEM, VMEM] + [ANY] * rows,
        out_specs=[VMEM] * (len(plan.moved) + 1),
        scratch_shapes=[
            pltpu.VMEM((rows, len(tiles) - 1, *block), own.dtype),
            pltpu.SemaphoreType.DMA((rows,)),
        ],
        compiler_params=SMALL,
        name="pick",
    )(table, squares, far_square, *square_panel)
    sends = {a: functools.partial(shifted, by=-a) for a in plan.moved}
    arrived = in_turn(
        dict(zip(plan.moved, picked)), sends, ordered(BACK_ORDER, plan.moved), BACK_WINDOW
    )
    return pl.pallas_call(
        functools.partial(cube_kernel, plan),
        out_shape=jax.ShapeDtypeStruct((1, slot_count, *block), jnp.float32),
        in_specs=[SMEM, VMEM, VMEM, VMEM] + [VMEM] * len(arrived),
        out_specs=VMEM,
        compiler_params=SMALL,
        name="cube",
    )(table, own, self_square, picked[-1], *[arrived[a] for a in plan.moved])


def solution(mesh):
    in_specs = (P(("row", "col"), None, None, None), P())
    out_specs = P(("row", "col"), None, None, None)
    return jax.shard_map(
        per_device, mesh=mesh, in_specs=in_specs, out_specs=out_specs, check_vma=False
    )
```

```python
import functools

import jax
import jax.numpy as jnp
from jax import lax
from jax.experimental import pallas as pl
from jax.experimental.pallas import tpu as pltpu
from jax.sharding import PartitionSpec as P

SIGNS = {1: 1, 2: 1, 3: -1, 4: 1, 5: -1, 6: -1, 7: 1}
PARENTS = {2: 1, -3: 1, -6: -5, 7: 4}
BACK_ORDER = [1, -1, 4, -4, 2, 5, -5, -2, 3, -3, 6, -6, 7, -7, 16]
BACK_WINDOW = 4


class Plan:
    def __init__(self, slot_count, grid_cols, grid_rows):
        half = (slot_count - 2) // 2
        self.slot_count, self.grid_cols, self.grid_rows = slot_count, grid_cols, grid_rows
        self.far = grid_cols // 2
        self.offsets = [0]
        for stride in range(1, half + 1):
            self.offsets += [stride, -stride]
        self.offsets.append(self.far)
        self.slot = {o: s for s, o in enumerate(self.offsets)}
        self.tiles = [0] + [SIGNS.get(d, 1) * d for d in range(1, half + 1)] + [self.far]
        self.tile = {d: t for t, d in enumerate(self.tiles)}
        near = [o for o in self.offsets if o not in (0, self.far)]
        self.left = {self.far: []}
        for d in self.tiles[1:-1]:
            self.left[d] = [a for a in near if a != d and self.near(a - d)]
        self.children = {p: [d for d in self.tiles if self.parent(d) == p] for p in self.tiles}
        self.carried = {}
        for d in self.tiles[1:]:
            wanted = {0} | set(self.left[d])
            for child in self.children[d]:
                wanted |= {0} | set(self.left[child])
            self.carried[d] = [a for a in self.offsets if a in wanted]
        self.edges = {self.far: []}
        for a in near:
            self.edges[a] = [b for b in near if b != a and (a - b) in self.tile]
        self.moved = [o for o in self.offsets if o != 0]

    def parent(self, d):
        p = PARENTS.get(d, 0)
        return p if d != 0 and p in self.tiles else (0 if d != 0 else None)

    def near(self, o):
        return o in self.slot and o != self.far

    def row_id(self, rank, col):
        return rank * self.grid_cols + lax.rem(col + 2 * self.grid_cols, self.grid_cols)


def shifted(value, by):
    length = lax.axis_size("col")
    return lax.ppermute(value, "col", [(i, (i + by) % length) for i in range(length)])


def in_turn(values, sends, order, window):
    results, last = {}, []
    for key in order:
        value = values[key]
        if len(last) >= window:
            value, _ = lax.optimization_barrier((value, last[-window]))
        results[key] = sends[key](value)
        last.append(results[key])
    return results


def ordered(preferred, keys):
    return [k for k in preferred if k in keys] + [k for k in keys if k not in preferred]


def nn(a, b):
    return lax.dot_general(a, b, (((1,), (0,)), ((), ())), preferred_element_type=jnp.float32)


def nt(a, b):
    return lax.dot_general(a, b, (((1,), (1,)), ((), ())), preferred_element_type=jnp.float32)


def tn(a, b):
    return lax.dot_general(a, b, (((0,), (0,)), ((), ())), preferred_element_type=jnp.float32)


def from_chip(block, step):
    length = lax.axis_size("row")
    chips = length // 2
    pairs = [(2 * x + h, 2 * ((x + step) % chips) + h) for x in range(chips) for h in range(2)]
    return lax.ppermute(block, "row", pairs)


def from_core(block):
    return lax.ppermute(block, "row", [(i, i ^ 1) for i in range(lax.axis_size("row"))])


def gather_rows(block):
    chips = lax.axis_size("row") // 2
    same = [block] + [None] * (chips - 1)
    same[1], same[chips - 1] = from_chip(block, 1), from_chip(block, chips - 1)
    for step in range(2, chips - 1):
        held, _ = lax.optimization_barrier((block, same[step - 1]))
        same[step] = from_chip(held, step)
    out = []
    for piece in same:
        out += [piece, from_core(piece)]
    return out


def piece_rank(plan, my_row, index):
    chips = plan.grid_rows // 2
    x = lax.rem(my_row // 2 - index // 2 + chips, chips)
    core = lax.rem(my_row, 2)
    if index % 2:
        core = 1 - core
    return 2 * x + core


def land(plan, my_row, pieces, panel, sems):
    copies = []
    for index, piece in enumerate(pieces):
        copy = pltpu.make_async_copy(piece, panel.at[piece_rank(plan, my_row, index)], sems.at[index])
        copy.start()
        copies.append(copy)
    return copies


def pack_kernel(choices, source, *outs):
    for out, choice in zip(outs, choices):
        for p, s in enumerate(choice):
            out[p] = source[s]


def pack(source, choices):
    return pl.pallas_call(
        functools.partial(pack_kernel, choices),
        out_shape=[jax.ShapeDtypeStruct((len(c), *source.shape[1:]), source.dtype) for c in choices],
        in_specs=[VMEM],
        out_specs=[VMEM] * len(choices),
        compiler_params=SMALL,
        name="pack",
    )(source)


def square_kernel(plan, *refs):
    cols, own = refs[0], refs[1]
    n_left = len(plan.tiles) - 1
    pieces = refs[2 + n_left:2 + n_left + plan.grid_rows]
    rest = refs[2 + n_left + plan.grid_rows:]
    out, far_out, self_square, panel, total, sems, left_sems = rest[:7]
    lefts = dict(zip(plan.tiles[1:], rest[7:]))
    n = plan.slot_count
    my_row, my_col = lax.axis_index("row"), lax.axis_index("col")
    copies = land(plan, my_row, pieces, panel, sems)
    for t in range(n_left):
        copy = pltpu.make_async_copy(refs[2 + t], rest[7 + t], left_sems.at[t])
        copy.start()
        copies.append(copy)
    acc = nt(own[0], own[0])
    for s in range(1, n):
        acc = acc + nt(own[s], own[s])
    self_square[...] = acc
    out[0] = acc.astype(out.dtype)
    for copy in copies:
        copy.wait()
    for t, d in enumerate(plan.tiles):
        if d == 0:
            continue
        left = lefts[d]
        i = plan.row_id(my_row, my_col - d)
        j = cols[i * n + plan.slot[d]]
        rank = j // plan.grid_cols
        back = plan.slot[-d] if d != plan.far else plan.slot[d]
        total[...] = nt(left[plan.carried[d].index(0)], panel[rank, back]) + tn(panel[rank, back], panel[rank, 0])
        for a in plan.left[d]:
            p = plan.carried[d].index(a)
            k = cols[i * n + plan.slot[a]]
            u = plan.slot[a - d]

            @pl.when(cols[j * n + u] == k)
            def _():
                total[...] += nt(left[p], panel[rank, u])

        if d == plan.far:
            far_out[0] = total[...].astype(out.dtype)
        else:
            out[t] = total[...].astype(out.dtype)


def pick_kernel(plan, *refs):
    cols, own, far = refs[0], refs[1], refs[2]
    pieces = refs[3:3 + plan.grid_rows]
    rest = refs[3 + plan.grid_rows:]
    n_out = len(plan.moved) + 1
    outs, (panel, sems) = rest[:n_out], rest[n_out:]
    n = plan.slot_count
    my_row, my_col = lax.axis_index("row"), lax.axis_index("col")
    copies = land(plan, my_row, pieces, panel, sems)
    for copy in copies:
        copy.wait()
    for out, a in zip(outs, plan.moved):
        i = plan.row_id(my_row, my_col - a)
        k = cols[i * n + plan.slot[a]]
        out[0] = panel[k // plan.grid_cols, 0]
        p = 1
        if a == plan.far:
            out[p] = far[0]
        elif a in plan.tile:
            out[p] = own[plan.tile[a]]
            p += 1
        for b in plan.edges[a]:
            j = cols[i * n + plan.slot[b]]
            out[p] = panel[j // plan.grid_cols, plan.tile[a - b]]
            p += 1
    i = plan.row_id(my_row, my_col)
    for p, d in enumerate(plan.tiles[1:-1]):
        j = cols[i * n + plan.slot[-d]]
        outs[-1][p] = panel[j // plan.grid_cols, plan.tile[d]]


def message_size(plan, a):
    return 1 + (1 if a in plan.tile else 0) + len(plan.edges[a])


def cube_kernel(plan, *refs):
    cols, own, self_square, local = refs[:4]
    arrived = dict(zip(plan.moved, refs[4:4 + len(plan.moved)]))
    out = refs[4 + len(plan.moved)]
    n = plan.slot_count
    my_row, my_col = lax.axis_index("row"), lax.axis_index("col")
    i = plan.row_id(my_row, my_col)
    s_self = self_square[...]
    acc = nn(own[0], s_self.astype(own.dtype))
    for a in plan.moved:
        t = plan.slot[a]
        diagonal = arrived[a][0]
        if a in plan.tile:
            s_ia = arrived[a][1]
            acc = acc + nt(own[t], s_ia)
            cube = nn(own[0], s_ia) + nn(own[t], diagonal)
            mine = s_ia.astype(jnp.float32)
        else:
            s_ai = local[plan.tile[-a] - 1]
            acc = acc + nn(own[t], s_ai)
            cube = nt(own[0], s_ai) + nn(own[t], diagonal)
            mine = s_ai.astype(jnp.float32).T
        out[0, t] = 3.0 * mine - 2.0 * cube
    out[0, 0] = 3.0 * s_self - 2.0 * acc
    for a in plan.moved:
        p = 2 if a in plan.tile else 1
        for b in plan.edges[a]:
            k, j = cols[i * n + plan.slot[a]], cols[i * n + plan.slot[b]]

            @pl.when(cols[j * n + plan.slot[a - b]] == k)
            def _():
                edge = arrived[a][p]
                ta, tb = plan.slot[a], plan.slot[b]
                out[0, tb] += -2.0 * nt(own[ta], edge)
                out[0, ta] += -2.0 * nn(own[tb], edge)

            p += 1


VMEM = pl.BlockSpec(memory_space=pltpu.VMEM)
SMEM = pl.BlockSpec(memory_space=pltpu.SMEM)
ANY = pl.BlockSpec(memory_space=pl.ANY)
SMALL = pltpu.CompilerParams(vmem_limit_bytes=12 << 20)


def per_device(density, cols):
    slot_count, size = density.shape[1], density.shape[2]
    plan = Plan(slot_count, lax.axis_size("col"), lax.axis_size("row"))
    own = density[0]
    table = cols.reshape(-1)
    block = (size, size)
    rows, tiles = plan.grid_rows, plan.tiles
    sizes = {d: len(plan.carried[d]) for d in tiles[1:]}
    panel = gather_rows(own)
    lefts = {}

    def hand_on(source, at, held):
        children = plan.children[at]
        choices = [[held.index(a) for a in plan.carried[d]] for d in children]
        for d, message in zip(children, pack(source, choices)):
            lefts[d] = shifted(message, d - at)

    hand_on(own, 0, plan.offsets)
    for d in [d for d in tiles[1:] if plan.children[d]]:
        hand_on(lefts[d], d, plan.carried[d])
    squares, far_square, self_square = pl.pallas_call(
        functools.partial(square_kernel, plan),
        out_shape=[
            jax.ShapeDtypeStruct((len(tiles) - 1, *block), own.dtype),
            jax.ShapeDtypeStruct((1, *block), own.dtype),
            jax.ShapeDtypeStruct(block, jnp.float32),
        ],
        in_specs=[SMEM, VMEM] + [ANY] * len(lefts) + [ANY] * rows,
        out_specs=[VMEM, VMEM, VMEM],
        scratch_shapes=[
            pltpu.VMEM((rows, slot_count, *block), own.dtype),
            pltpu.VMEM(block, jnp.float32),
            pltpu.SemaphoreType.DMA((rows,)),
            pltpu.SemaphoreType.DMA((len(lefts),)),
        ] + [pltpu.VMEM((sizes[d], *block), own.dtype) for d in tiles[1:]],
        compiler_params=SMALL,
        name="square",
    )(table, own, *[lefts[d] for d in tiles[1:]], *panel)
    square_panel = gather_rows(squares)
    picked = pl.pallas_call(
        functools.partial(pick_kernel, plan),
        out_shape=[
            jax.ShapeDtypeStruct((message_size(plan, a), *block), own.dtype) for a in plan.moved
        ] + [jax.ShapeDtypeStruct((len(tiles) - 2, *block), own.dtype)],
        in_specs=[SMEM, VMEM, VMEM] + [ANY] * rows,
        out_specs=[VMEM] * (len(plan.moved) + 1),
        scratch_shapes=[
            pltpu.VMEM((rows, len(tiles) - 1, *block), own.dtype),
            pltpu.SemaphoreType.DMA((rows,)),
        ],
        compiler_params=SMALL,
        name="pick",
    )(table, squares, far_square, *square_panel)
    sends = {a: functools.partial(shifted, by=-a) for a in plan.moved}
    arrived = in_turn(
        dict(zip(plan.moved, picked)), sends, ordered(BACK_ORDER, plan.moved), BACK_WINDOW
    )
    return pl.pallas_call(
        functools.partial(cube_kernel, plan),
        out_shape=jax.ShapeDtypeStruct((1, slot_count, *block), jnp.float32),
        in_specs=[SMEM, VMEM, VMEM, VMEM] + [VMEM] * len(arrived),
        out_specs=VMEM,
        compiler_params=SMALL,
        name="cube",
    )(table, own, self_square, picked[-1], *[arrived[a] for a in plan.moved])


def solution(mesh):
    in_specs = (P(("row", "col"), None, None, None), P())
    out_specs = P(("row", "col"), None, None, None)
    return jax.shard_map(
        per_device, mesh=mesh, in_specs=in_specs, out_specs=out_specs, check_vma=False
    )
```

```python
import functools

import jax
import jax.numpy as jnp
from jax import lax
from jax.experimental import pallas as pl
from jax.experimental.pallas import tpu as pltpu
from jax.sharding import PartitionSpec as P

SIGNS = {1: 1, 2: 1, 3: -1, 4: 1, 5: -1, 6: -1, 7: 1}
ROUNDS = [[(1, 5), (-1, -5), (3, 7), (-3, -7)], [(2, 6), (-2, -6)]]
STEP = 4
LONG = {4: [4, 5, 3, 6], -4: [-4, -3, -5, -2], 8: [7], -8: [-7, -6]}
SHORT = [1, -1, 2]


class Plan:
    def __init__(self, slot_count, grid_cols, grid_rows):
        half = (slot_count - 2) // 2
        self.slot_count, self.grid_cols, self.grid_rows = slot_count, grid_cols, grid_rows
        self.far = grid_cols // 2
        self.offsets = [0]
        for stride in range(1, half + 1):
            self.offsets += [stride, -stride]
        self.offsets.append(self.far)
        self.slot = {o: s for s, o in enumerate(self.offsets)}
        self.moved = self.offsets[1:]
        near = self.offsets[1:-1]
        self.kept = [0] + [SIGNS.get(d, 1) * d for d in range(1, half + 1)]
        self.place = {d: p for p, d in enumerate(self.kept)}
        self.edges = {self.far: []}
        for a in near:
            self.edges[a] = [b for b in near if b != a and (a - b) in self.place]
        self.size = {a: 1 + len(self.edges[a]) for a in self.moved}
        self.bundles, self.onward = {}, []
        for number, pairs in enumerate(ROUNDS):
            legs = {STEP: [], -STEP: []}
            if number == 0:
                legs = {STEP: [STEP], -STEP: [-STEP]}
            for f, a in pairs:
                self.bundles[f] = [f, a]
                legs[a - f].append(a)
            self.onward.append(legs)
        self.long = {e: [a for a in LONG[e] if a in self.slot] for e in LONG}
        relayed = [a for e in LONG for a in self.long[e]]
        self.short = {f: [f] + [a for e in LONG for a in self.long[e] if a - e == f] for f in SHORT}
        self.alone = [a for a in self.moved if a not in relayed and a not in SHORT]

    def back(self, a):
        return self.slot[a if a == self.far else -a]

    def row_id(self, rank, col):
        return rank * self.grid_cols + lax.rem(col + 2 * self.grid_cols, self.grid_cols)


def shifted(value, by):
    length = lax.axis_size("col")
    return lax.ppermute(value, "col", [(i, (i + by) % length) for i in range(length)])


def after(value, *others):
    return lax.optimization_barrier((value, *others))[0]


def nn(a, b):
    return lax.dot_general(a, b, (((1,), (0,)), ((), ())), preferred_element_type=jnp.float32)


def nt(a, b):
    return lax.dot_general(a, b, (((1,), (1,)), ((), ())), preferred_element_type=jnp.float32)


def from_chip(block, step):
    length = lax.axis_size("row")
    chips = length // 2
    pairs = [(2 * x + h, 2 * ((x + step) % chips) + h) for x in range(chips) for h in range(2)]
    return lax.ppermute(block, "row", pairs)


def from_core(block):
    return lax.ppermute(block, "row", [(i, i ^ 1) for i in range(lax.axis_size("row"))])


def gather_rows(block):
    chips = lax.axis_size("row") // 2
    same = [block] + [None] * (chips - 1)
    same[1], same[chips - 1] = from_chip(block, 1), from_chip(block, chips - 1)
    for step in range(2, chips - 1):
        held, _ = lax.optimization_barrier((block, same[step - 1]))
        same[step] = from_chip(held, step)
    out = []
    for piece in same:
        out += [piece, from_core(piece)]
    return out


def piece_rank(plan, my_row, index):
    chips = plan.grid_rows // 2
    x = lax.rem(my_row // 2 - index // 2 + chips, chips)
    core = lax.rem(my_row, 2)
    if index % 2:
        core = 1 - core
    return 2 * x + core


def land(plan, my_row, pieces, panel, sems):
    copies = []
    for index, piece in enumerate(pieces):
        copy = pltpu.make_async_copy(piece, panel.at[piece_rank(plan, my_row, index)], sems.at[index])
        copy.start()
        copies.append(copy)
    return copies


def keep_kernel(plan, own, out):
    for p, d in enumerate(plan.kept):
        out[p] = own[plan.slot[-d]]


def pick_kernel(plan, *refs):
    cols, pieces = refs[0], refs[1:1 + plan.grid_rows]
    outs, (panel, sems) = refs[1 + plan.grid_rows:-2], refs[-2:]
    n = plan.slot_count
    my_row, my_col = lax.axis_index("row"), lax.axis_index("col")
    for copy in land(plan, my_row, pieces, panel, sems):
        copy.wait()
    for out, group in zip(outs, pick_groups(plan)):
        at = 0
        for a in group:
            i = plan.row_id(my_row, my_col - a)
            rank = cols[i * n + plan.slot[a]] // plan.grid_cols
            out[at] = panel[rank, 0]
            for p, b in enumerate(plan.edges[a]):
                out[at + p + 1] = panel[rank, plan.place[a - b]]
            at += plan.size[a]


def pick_groups(plan):
    return list(plan.bundles.values()) + [[STEP], [-STEP], [plan.far]]


def total_size(plan, group):
    return sum(plan.size[a] for a in group)


def start_of(plan, group, a):
    return total_size(plan, group[:group.index(a)])


def onward_kernel(plan, number, held, *refs):
    outs = refs[len(held):]
    for out, group in zip(outs, plan.onward[number].values()):
        at = 0
        for a in group:
            source = [a in h for h in held].index(True)
            first = start_of(plan, held[source], a)
            for p in range(plan.size[a]):
                out[at + p] = refs[source][first + p]
            at += plan.size[a]


class Part:
    def __init__(self, ref, first):
        self.ref, self.first = ref, first

    def __getitem__(self, p):
        return self.ref[self.first + p]


def product_kernel(plan, held, *refs):
    cols, own = refs[:2]
    arrived = {}
    for ref, group in zip(refs[2:2 + len(held)], held):
        for a in group:
            arrived[a] = Part(ref, start_of(plan, group, a))
    away, self_new, total, half = refs[2 + len(held):]
    n = plan.slot_count
    i = plan.row_id(lax.axis_index("row"), lax.axis_index("col"))

    def add_edges(left, scale):
        for a in plan.moved:
            for p, b in enumerate(plan.edges[a]):
                ta, tb = plan.slot[a], plan.slot[b]
                k, j = cols[i * n + ta], cols[i * n + tb]

                @pl.when(cols[k * n + plan.slot[b - a]] == j)
                def _():
                    edge = arrived[a][p + 1]
                    total[tb] += scale * nn(left[ta], edge)
                    total[ta] += scale * nt(left[tb], edge)

    acc = nt(own[0], own[0])
    for s in range(1, n):
        acc = acc + nt(own[s], own[s])
    total[0] = acc
    half[0] = acc.astype(half.dtype)
    for a in plan.moved:
        t = plan.slot[a]
        total[t] = nn(own[0], own[t]) + nn(own[t], arrived[a][0])
    add_edges(own, 1.0)
    for t in range(1, n):
        half[t] = total[t].astype(half.dtype)
    acc = nt(own[0], half[0])
    for s in range(1, n):
        acc = acc + nt(own[s], half[s])
    self_new[...] = 3.0 * total[0] - 2.0 * acc
    for a in plan.moved:
        t = plan.slot[a]
        cube = nn(half[0], own[t]) + nn(half[t], arrived[a][0])
        total[t] = 3.0 * total[t] - 2.0 * cube
    add_edges(half, -2.0)
    for t in range(1, n):
        away[t - 1] = total[t].astype(away.dtype)


def home_kernel(plan, *refs):
    cols, pieces, outs = refs[0], refs[1:1 + plan.grid_rows], refs[1 + plan.grid_rows:]
    n = plan.slot_count
    my_row, my_col = lax.axis_index("row"), lax.axis_index("col")
    for out, group in zip(outs, home_groups(plan)):
        for p, a in enumerate(group):
            i = plan.row_id(my_row, my_col - a)
            rank = cols[i * n + plan.slot[a]] // plan.grid_cols
            for index, piece in enumerate(pieces):

                @pl.when(rank == piece_rank(plan, my_row, index))
                def _():
                    out[p] = piece[plan.back(a) - 1]


def home_groups(plan):
    return [plan.long[e] for e in LONG] + [SHORT] + [[a] for a in plan.alone]


def relay_kernel(plan, *refs):
    longs, near = dict(zip(LONG, refs)), refs[len(LONG)]
    for out, f in zip(refs[len(LONG) + 1:], SHORT):
        out[0] = near[SHORT.index(f)]
        for p, a in enumerate(plan.short[f][1:]):
            e = a - f
            out[p + 1] = longs[e][plan.long[e].index(a)]


def finish_kernel(where, self_new, *refs):
    out = refs[-1]
    out[0, 0] = self_new[...]
    for t, (source, p) in where.items():
        out[0, t] = refs[source][p].astype(jnp.float32).T


VMEM = pl.BlockSpec(memory_space=pltpu.VMEM)
SMEM = pl.BlockSpec(memory_space=pltpu.SMEM)
ANY = pl.BlockSpec(memory_space=pl.ANY)
SMALL = pltpu.CompilerParams(vmem_limit_bytes=12 << 20)


def call(kernel, name, args, specs, outs, scratch=()):
    return pl.pallas_call(
        kernel,
        out_shape=[jax.ShapeDtypeStruct(shape, dtype) for shape, dtype in outs],
        in_specs=specs,
        out_specs=[VMEM] * len(outs),
        scratch_shapes=list(scratch),
        compiler_params=SMALL,
        name=name,
    )(*args)


def per_device(density, cols):
    slot_count, block = density.shape[1], density.shape[2:]
    plan = Plan(slot_count, lax.axis_size("col"), lax.axis_size("row"))
    own, dtype, rows = density[0], density.dtype, plan.grid_rows
    table = cols.reshape(-1)
    n_moved = len(plan.moved)

    def panel_scratch(blocks):
        return [pltpu.VMEM((rows, blocks, *block), dtype), pltpu.SemaphoreType.DMA((rows,))]

    n_kept = len(plan.kept)
    (kept,) = call(
        functools.partial(keep_kernel, plan), "keep", [own], [VMEM], [((n_kept, *block), dtype)]
    )
    groups = pick_groups(plan)
    picked = call(
        functools.partial(pick_kernel, plan), "pick",
        [table, *gather_rows(kept)], [SMEM] + [ANY] * rows,
        [((total_size(plan, g), *block), dtype) for g in groups],
        panel_scratch(n_kept),
    )
    *bundles, up, down, far = picked
    far = shifted(far, -plan.far)
    came, held, last = [], [], []
    for number, pairs in enumerate(ROUNDS):
        arrays, contents = [], []
        for index, (f, a) in enumerate(pairs):
            message = bundles[list(plan.bundles).index(f)]
            if last:
                message = after(message, last[index], far)
            arrays.append(shifted(message, -f))
            contents.append(plan.bundles[f])
        last = arrays
        came, held = came + arrays, held + contents
        if number == 0:
            arrays, contents = arrays + [up, down], contents + [[STEP], [-STEP]]
        legs = plan.onward[number]
        joined = call(
            functools.partial(onward_kernel, plan, number, contents), "onward",
            arrays, [VMEM] * len(arrays),
            [((total_size(plan, g), *block), dtype) for g in legs.values()],
        )
        came += [shifted(m, -e) for m, e in zip(joined, legs)]
        held += list(legs.values())
    came.append(far)
    held = [[f for f in g] for g in held] + [[plan.far]]
    away, self_new = call(
        functools.partial(product_kernel, plan, held), "product",
        [table, own, *came], [SMEM] + [VMEM] * (1 + len(came)),
        [((n_moved, *block), dtype), (block, jnp.float32)],
        [pltpu.VMEM((slot_count, *block), jnp.float32), pltpu.VMEM((slot_count, *block), dtype)],
    )
    groups = home_groups(plan)
    homing = call(
        functools.partial(home_kernel, plan), "home",
        [table, *gather_rows(away)], [SMEM] + [VMEM] * rows,
        [((len(g), *block), dtype) for g in groups],
    )
    n_long = len(LONG)
    longs = [shifted(m, -e) for m, e in zip(homing, LONG)]
    alone = [shifted(m, -a) for m, a in zip(homing[n_long + 1:], plan.alone)]
    longs = list(lax.optimization_barrier((*longs, *alone)))
    longs, alone = longs[:n_long], longs[n_long:]
    relayed = call(
        functools.partial(relay_kernel, plan), "relay",
        [*longs, homing[n_long]], [VMEM] * (n_long + 1),
        [((len(plan.short[f]), *block), dtype) for f in SHORT],
    )
    shorts = [shifted(m, -f) for m, f in zip(relayed, SHORT)]
    came = longs + alone + shorts
    where = {}
    for source, e in enumerate(LONG):
        if e in plan.long[e]:
            where[plan.slot[e]] = (source, plan.long[e].index(e))
    for source, a in enumerate(plan.alone):
        where[plan.slot[a]] = (n_long + source, 0)
    for source, f in enumerate(SHORT):
        for p, a in enumerate(plan.short[f]):
            where[plan.slot[a]] = (n_long + len(alone) + source, p)
    (new,) = call(
        functools.partial(finish_kernel, where), "finish",
        [self_new, *came], [VMEM] * (1 + len(came)),
        [((1, slot_count, *block), jnp.float32)],
    )
    return new


def solution(mesh):
    in_specs = (P(("row", "col"), None, None, None), P())
    out_specs = P(("row", "col"), None, None, None)
    return jax.shard_map(
        per_device, mesh=mesh, in_specs=in_specs, out_specs=out_specs, check_vma=False
    )
```

```python
import functools

import jax
import jax.numpy as jnp
from jax import lax
from jax.experimental import pallas as pl
from jax.experimental.pallas import tpu as pltpu
from jax.sharding import PartitionSpec as P

SIGNS = {1: 1, 2: 1, 3: -1, 4: 1, 5: -1, 6: -1, 7: 1}
FIRST = {1: [1, 5], -1: [-1, -5], 2: [2, 6], -2: [-2, -6], 4: [4, 7], -4: [-4, -7]}
THEN = [({4: [5], -4: [-5]}, (1, -1)), ({3: [3, 7], -3: [-3, -7]}, (4, -4)), ({4: [6], -4: [-6]}, (2, -2))]
LONG = {4: [4, 5, 3, 6], -4: [-4, -3, -5, -2], 8: [7], -8: [-7, -6]}
SHORT = [1, -1, 2]


class Plan:
    def __init__(self, slot_count, grid_cols, grid_rows):
        half = (slot_count - 2) // 2
        self.slot_count, self.grid_cols, self.grid_rows = slot_count, grid_cols, grid_rows
        self.far = grid_cols // 2
        self.offsets = [0]
        for stride in range(1, half + 1):
            self.offsets += [stride, -stride]
        self.offsets.append(self.far)
        self.slot = {o: s for s, o in enumerate(self.offsets)}
        self.moved = self.offsets[1:]
        near = self.offsets[1:-1]
        self.kept = [0] + [SIGNS.get(d, 1) * d for d in range(1, half + 1)]
        self.place = {d: p for p, d in enumerate(self.kept)}
        self.edges = {self.far: []}
        for a in near:
            self.edges[a] = [b for b in near if b != a and (a - b) in self.place]
        self.size = {a: 1 + len(self.edges[a]) for a in near}
        self.size[self.far] = 2
        self.near_moved = near
        self.long = {e: [a for a in LONG[e] if a in self.slot] for e in LONG}
        relayed = [a for e in LONG for a in self.long[e]]
        self.short = {f: [f] + [a for e in LONG for a in self.long[e] if a - e == f] for f in SHORT}
        self.alone = [a for a in near if a not in relayed and a not in SHORT]

    def row_id(self, rank, col):
        return rank * self.grid_cols + lax.rem(col + 2 * self.grid_cols, self.grid_cols)


def shifted(value, by):
    length = lax.axis_size("col")
    return lax.ppermute(value, "col", [(i, (i + by) % length) for i in range(length)])


def after(value, *others):
    return lax.optimization_barrier((value, *others))[0]


def nn(a, b):
    return lax.dot_general(a, b, (((1,), (0,)), ((), ())), preferred_element_type=jnp.float32)


def nt(a, b):
    return lax.dot_general(a, b, (((1,), (1,)), ((), ())), preferred_element_type=jnp.float32)


def from_chip(block, step):
    length = lax.axis_size("row")
    chips = length // 2
    pairs = [(2 * x + h, 2 * ((x + step) % chips) + h) for x in range(chips) for h in range(2)]
    return lax.ppermute(block, "row", pairs)


def from_core(block):
    return lax.ppermute(block, "row", [(i, i ^ 1) for i in range(lax.axis_size("row"))])


def gather_rows(block):
    chips = lax.axis_size("row") // 2
    same = [block] + [None] * (chips - 1)
    same[1], same[chips - 1] = from_chip(block, 1), from_chip(block, chips - 1)
    for step in range(2, chips - 1):
        held, _ = lax.optimization_barrier((block, same[step - 1]))
        same[step] = from_chip(held, step)
    out = []
    for piece in same:
        out += [piece, from_core(piece)]
    return out


def piece_rank(plan, my_row, index):
    chips = plan.grid_rows // 2
    x = lax.rem(my_row // 2 - index // 2 + chips, chips)
    core = lax.rem(my_row, 2)
    if index % 2:
        core = 1 - core
    return 2 * x + core


def land(plan, my_row, pieces, panel, sems):
    copies = []
    for index, piece in enumerate(pieces):
        copy = pltpu.make_async_copy(piece, panel.at[piece_rank(plan, my_row, index)], sems.at[index])
        copy.start()
        copies.append(copy)
    return copies


def keep_kernel(plan, own, out):
    for p, d in enumerate(plan.kept):
        out[p] = own[plan.slot[-d]]
    square = nt(own[0], own[0])
    for s in range(1, plan.slot_count):
        square = square + nt(own[s], own[s])
    out[len(plan.kept)] = square.astype(out.dtype)


def pick_kernel(plan, *refs):
    cols, pieces = refs[0], refs[1:1 + plan.grid_rows]
    outs, (panel, sems) = refs[1 + plan.grid_rows:-2], refs[-2:]
    n = plan.slot_count
    my_row, my_col = lax.axis_index("row"), lax.axis_index("col")
    for copy in land(plan, my_row, pieces, panel, sems):
        copy.wait()
    for out, group in zip(outs, pick_groups(plan)):
        at = 0
        for a in group:
            i = plan.row_id(my_row, my_col - a)
            rank = cols[i * n + plan.slot[a]] // plan.grid_cols
            out[at] = panel[rank, 0]
            if a == plan.far:
                out[at + 1] = panel[rank, len(plan.kept)]
            for p, b in enumerate(plan.edges[a]):
                out[at + p + 1] = panel[rank, plan.place[a - b]]
            at += plan.size[a]


def pick_groups(plan):
    return [[plan.far]] + list(FIRST.values()) + [[3], [-3]]


def total_size(plan, group):
    return sum(plan.size[a] for a in group)


def start_of(plan, group, a):
    return total_size(plan, group[:group.index(a)])


def join_kernel(plan, held, groups, *refs):
    for out, group in zip(refs[len(held):], groups):
        at = 0
        for a in group:
            source = [a in h for h in held].index(True)
            first = start_of(plan, held[source], a)
            for p in range(plan.size[a]):
                out[at + p] = refs[source][first + p]
            at += plan.size[a]


def join(plan, arrays, held, groups):
    block, dtype = arrays[0].shape[1:], arrays[0].dtype
    return call(
        functools.partial(join_kernel, plan, held, groups), "join",
        arrays, [VMEM] * len(arrays),
        [((total_size(plan, g), *block), dtype) for g in groups],
    )


class Part:
    def __init__(self, ref, first):
        self.ref, self.first = ref, first

    def __getitem__(self, p):
        return self.ref[self.first + p]


def product_kernel(plan, held, *refs):
    cols, own = refs[:2]
    arrived = {}
    for ref, group in zip(refs[2:2 + len(held)], held):
        for a in group:
            arrived[a] = Part(ref, start_of(plan, group, a))
    away, self_new, total, half = refs[2 + len(held):]
    n = plan.slot_count
    i = plan.row_id(lax.axis_index("row"), lax.axis_index("col"))

    def add_edges(left, scale):
        for a in plan.moved:
            for p, b in enumerate(plan.edges[a]):
                ta, tb = plan.slot[a], plan.slot[b]
                k, j = cols[i * n + ta], cols[i * n + tb]

                @pl.when(cols[k * n + plan.slot[b - a]] == j)
                def _():
                    edge = arrived[a][p + 1]
                    total[tb] += scale * nn(left[ta], edge)
                    total[ta] += scale * nt(left[tb], edge)

    acc = nt(own[0], own[0])
    for s in range(1, n):
        acc = acc + nt(own[s], own[s])
    total[0] = acc
    half[0] = acc.astype(half.dtype)
    for a in plan.moved:
        t = plan.slot[a]
        total[t] = nn(own[0], own[t]) + nn(own[t], arrived[a][0])
    add_edges(own, 1.0)
    for t in range(1, n):
        half[t] = total[t].astype(half.dtype)
    acc = nt(own[0], half[0])
    for s in range(1, n):
        acc = acc + nt(own[s], half[s])
    self_new[0] = 3.0 * total[0] - 2.0 * acc
    t = plan.slot[plan.far]
    cube = nn(own[0], half[t]) + nn(own[t], arrived[plan.far][1])
    self_new[1] = 3.0 * total[t] - 2.0 * cube
    for a in plan.near_moved:
        t = plan.slot[a]
        cube = nn(half[0], own[t]) + nn(half[t], arrived[a][0])
        total[t] = 3.0 * total[t] - 2.0 * cube
    add_edges(half, -2.0)
    for a in plan.near_moved:
        t = plan.slot[a]
        away[t - 1] = total[t].astype(away.dtype)


def home_kernel(plan, *refs):
    cols, pieces, outs = refs[0], refs[1:1 + plan.grid_rows], refs[1 + plan.grid_rows:]
    n = plan.slot_count
    my_row, my_col = lax.axis_index("row"), lax.axis_index("col")
    for out, group in zip(outs, home_groups(plan)):
        for p, a in enumerate(group):
            i = plan.row_id(my_row, my_col - a)
            rank = cols[i * n + plan.slot[a]] // plan.grid_cols
            for index, piece in enumerate(pieces):

                @pl.when(rank == piece_rank(plan, my_row, index))
                def _():
                    out[p] = piece[plan.slot[-a] - 1]


def home_groups(plan):
    return [plan.long[e] for e in LONG] + [SHORT] + [[a] for a in plan.alone]


def relay_kernel(plan, *refs):
    longs, near = dict(zip(LONG, refs)), refs[len(LONG)]
    for out, f in zip(refs[len(LONG) + 1:], SHORT):
        out[0] = near[SHORT.index(f)]
        for p, a in enumerate(plan.short[f][1:]):
            e = a - f
            out[p + 1] = longs[e][plan.long[e].index(a)]


def finish_kernel(where, self_new, *refs):
    out = refs[-1]
    out[0, 0] = self_new[0]
    out[0, out.shape[1] - 1] = self_new[1]
    for t, (source, p) in where.items():
        out[0, t] = refs[source][p].astype(jnp.float32).T


VMEM = pl.BlockSpec(memory_space=pltpu.VMEM)
SMEM = pl.BlockSpec(memory_space=pltpu.SMEM)
ANY = pl.BlockSpec(memory_space=pl.ANY)
SMALL = pltpu.CompilerParams(vmem_limit_bytes=12 << 20)


def call(kernel, name, args, specs, outs, scratch=()):
    return pl.pallas_call(
        kernel,
        out_shape=[jax.ShapeDtypeStruct(shape, dtype) for shape, dtype in outs],
        in_specs=specs,
        out_specs=[VMEM] * len(outs),
        scratch_shapes=list(scratch),
        compiler_params=SMALL,
        name=name,
    )(*args)


def per_device(density, cols):
    slot_count, block = density.shape[1], density.shape[2:]
    plan = Plan(slot_count, lax.axis_size("col"), lax.axis_size("row"))
    own, dtype, rows = density[0], density.dtype, plan.grid_rows
    table = cols.reshape(-1)

    def panel_scratch(blocks):
        return [pltpu.VMEM((rows, blocks, *block), dtype), pltpu.SemaphoreType.DMA((rows,))]

    n_kept = len(plan.kept) + 1
    (kept,) = call(
        functools.partial(keep_kernel, plan), "keep", [own], [VMEM], [((n_kept, *block), dtype)]
    )
    groups = pick_groups(plan)
    far, *first, three, minus_three = call(
        functools.partial(pick_kernel, plan), "pick",
        [table, *gather_rows(kept)], [SMEM] + [ANY] * rows,
        [((total_size(plan, g), *block), dtype) for g in groups],
        panel_scratch(n_kept),
    )
    far = shifted(far, -plan.far)
    came = {}
    for f, message in zip(FIRST, first):
        if abs(f) == 4:
            message = after(message, far)
        came[f] = shifted(message, -f)
    waiting = {4: (three, [3]), -4: (minus_three, [-3])}
    second, held = [], list(FIRST.values())
    for bundles, sources in THEN:
        arrays, contents = [came[f] for f in sources], [FIRST[f] for f in sources]
        if 4 in sources:
            arrays[0] = after(arrays[0], came[2], came[-2])
        for f in sources:
            if f in waiting:
                arrays.append(waiting[f][0])
                contents.append(waiting[f][1])
        joined = join(plan, arrays, contents, list(bundles.values()))
        second += [shifted(m, -f) for f, m in zip(bundles, joined)]
        held += list(bundles.values())
    came = list(came.values()) + second + [far]
    held.append([plan.far])
    away, self_new = call(
        functools.partial(product_kernel, plan, held), "product",
        [table, own, *came], [SMEM] + [VMEM] * (1 + len(came)),
        [((len(plan.near_moved), *block), dtype), ((2, *block), jnp.float32)],
        [pltpu.VMEM((slot_count, *block), jnp.float32), pltpu.VMEM((slot_count, *block), dtype)],
    )
    groups = home_groups(plan)
    homing = call(
        functools.partial(home_kernel, plan), "home",
        [table, *gather_rows(away)], [SMEM] + [VMEM] * rows,
        [((len(g), *block), dtype) for g in groups],
    )
    n_long = len(LONG)
    longs = [shifted(m, -e) for m, e in zip(homing, LONG)]
    alone = [shifted(m, -a) for m, a in zip(homing[n_long + 1:], plan.alone)]
    longs = list(lax.optimization_barrier((*longs, *alone)))
    longs, alone = longs[:n_long], longs[n_long:]
    relayed = call(
        functools.partial(relay_kernel, plan), "relay",
        [*longs, homing[n_long]], [VMEM] * (n_long + 1),
        [((len(plan.short[f]), *block), dtype) for f in SHORT],
    )
    shorts = [shifted(m, -f) for m, f in zip(relayed, SHORT)]
    came = longs + alone + shorts
    where = {}
    for source, e in enumerate(LONG):
        if e in plan.long[e]:
            where[plan.slot[e]] = (source, plan.long[e].index(e))
    for source, a in enumerate(plan.alone):
        where[plan.slot[a]] = (n_long + source, 0)
    for source, f in enumerate(SHORT):
        for p, a in enumerate(plan.short[f]):
            where[plan.slot[a]] = (n_long + len(alone) + source, p)
    (new,) = call(
        functools.partial(finish_kernel, where), "finish",
        [self_new, *came], [VMEM] * (1 + len(came)),
        [((1, slot_count, *block), jnp.float32)],
    )
    return new


def solution(mesh):
    in_specs = (P(("row", "col"), None, None, None), P())
    out_specs = P(("row", "col"), None, None, None)
    return jax.shard_map(
        per_device, mesh=mesh, in_specs=in_specs, out_specs=out_specs, check_vma=False
    )
```

```python
import functools

import jax
import jax.numpy as jnp
from jax import lax
from jax.experimental import pallas as pl
from jax.experimental.pallas import tpu as pltpu
from jax.sharding import PartitionSpec as P

SIGNS = {1: 1, 2: 1, 3: -1, 4: 1, 5: -1, 6: -1, 7: 1}
FIRST = {1: [1, 5], -1: [-1, -5], 2: [2, 6], -2: [-2, -6], 4: [4, 7], -4: [-4, -7]}
THEN = [({4: [5], -4: [-5]}, (1, -1)), ({3: [3, 7], -3: [-3, -7]}, (4, -4)), ({4: [6], -4: [-6]}, (2, -2))]
LONG = {4: [4, 5, 3, 6], -4: [-4, -3, -5, -2], 8: [7], -8: [-7, -6]}
SHORT = [1, -1, 2]


class Plan:
    def __init__(self, slot_count, grid_cols, grid_rows):
        half = (slot_count - 2) // 2
        self.slot_count, self.grid_cols, self.grid_rows = slot_count, grid_cols, grid_rows
        self.far = grid_cols // 2
        self.offsets = [0]
        for stride in range(1, half + 1):
            self.offsets += [stride, -stride]
        self.offsets.append(self.far)
        self.slot = {o: s for s, o in enumerate(self.offsets)}
        self.moved = self.offsets[1:]
        near = self.offsets[1:-1]
        self.kept = [0] + [SIGNS.get(d, 1) * d for d in range(1, half + 1)]
        self.place = {d: p for p, d in enumerate(self.kept)}
        self.edges = {self.far: []}
        for a in near:
            self.edges[a] = [b for b in near if b != a and (a - b) in self.place]
        self.size = {a: 1 + len(self.edges[a]) for a in near}
        self.size[self.far] = 2
        self.near_moved = near
        self.long = {e: [a for a in LONG[e] if a in self.slot] for e in LONG}
        relayed = [a for e in LONG for a in self.long[e]]
        self.short = {f: [f] + [a for e in LONG for a in self.long[e] if a - e == f] for f in SHORT}
        self.alone = [a for a in near if a not in relayed and a not in SHORT]

    def row_id(self, rank, col):
        return rank * self.grid_cols + lax.rem(col + 2 * self.grid_cols, self.grid_cols)


def shifted(value, by):
    length = lax.axis_size("col")
    return lax.ppermute(value, "col", [(i, (i + by) % length) for i in range(length)])


def after(value, *others):
    return lax.optimization_barrier((value, *others))[0]


def nn(a, b):
    return lax.dot_general(a, b, (((1,), (0,)), ((), ())), preferred_element_type=jnp.float32)


def nt(a, b):
    return lax.dot_general(a, b, (((1,), (1,)), ((), ())), preferred_element_type=jnp.float32)


def from_chip(block, step):
    length = lax.axis_size("row")
    chips = length // 2
    pairs = [(2 * x + h, 2 * ((x + step) % chips) + h) for x in range(chips) for h in range(2)]
    return lax.ppermute(block, "row", pairs)


def from_core(block):
    return lax.ppermute(block, "row", [(i, i ^ 1) for i in range(lax.axis_size("row"))])


def gather_rows(block):
    half = block.shape[0] // 2
    ahead, behind = from_chip(block, 1), from_chip(block, -1)
    out = []
    for piece in (block, ahead, from_chip(ahead[:half], 1), from_chip(behind[half:], -1), behind):
        out += [piece, from_core(piece)]
    return out


def gather_small(block):
    chips = lax.axis_size("row") // 2
    same = [block] + [None] * (chips - 1)
    same[1], same[chips - 1] = from_chip(block, 1), from_chip(block, chips - 1)
    for step in range(2, chips - 1):
        held, _ = lax.optimization_barrier((block, same[step - 1]))
        same[step] = from_chip(held, step)
    out = []
    for piece in same:
        out += [piece, from_core(piece)]
    return out


def piece_rank(plan, my_row, index):
    chips = plan.grid_rows // 2
    x = lax.rem(my_row // 2 - index // 2 + chips, chips)
    core = lax.rem(my_row, 2)
    if index % 2:
        core = 1 - core
    return 2 * x + core


def land(plan, my_row, pieces, panel, sems):
    copies = []
    for index, piece in enumerate(pieces):
        copy = pltpu.make_async_copy(piece, panel.at[piece_rank(plan, my_row, index)], sems.at[index])
        copy.start()
        copies.append(copy)
    return copies


def keep_kernel(plan, own, out):
    for p, d in enumerate(plan.kept):
        out[p] = own[plan.slot[-d]]
    square = nt(own[0], own[0])
    for s in range(1, plan.slot_count):
        square = square + nt(own[s], own[s])
    out[len(plan.kept)] = square.astype(out.dtype)


class Joined:
    def __init__(self, refs):
        self.first, self.second = refs

    def __getitem__(self, p):
        n = self.first.shape[0]
        return self.first[p] if p < n else self.second[p - n]


def pick_kernel(plan, *refs):
    cols, pieces = refs[0], refs[1:1 + plan.grid_rows]
    outs, (panel, sems) = refs[1 + plan.grid_rows:-2], refs[-2:]
    n = plan.slot_count
    my_row, my_col = lax.axis_index("row"), lax.axis_index("col")
    for copy in land(plan, my_row, pieces, panel, sems):
        copy.wait()
    for out, group in zip(outs, pick_groups(plan)):
        at = 0
        for a in group:
            i = plan.row_id(my_row, my_col - a)
            rank = cols[i * n + plan.slot[a]] // plan.grid_cols
            out[at] = panel[rank, 0]
            if a == plan.far:
                out[at + 1] = panel[rank, len(plan.kept)]
            for p, b in enumerate(plan.edges[a]):
                out[at + p + 1] = panel[rank, plan.place[a - b]]
            at += plan.size[a]


def pick_groups(plan):
    return [[plan.far]] + list(FIRST.values()) + [[3], [-3]]


def total_size(plan, group):
    return sum(plan.size[a] for a in group)


def start_of(plan, group, a):
    return total_size(plan, group[:group.index(a)])


def join_kernel(plan, held, groups, *refs):
    for out, group in zip(refs[len(held):], groups):
        at = 0
        for a in group:
            source = [a in h for h in held].index(True)
            first = start_of(plan, held[source], a)
            for p in range(plan.size[a]):
                out[at + p] = refs[source][first + p]
            at += plan.size[a]


def join(plan, arrays, held, groups):
    block, dtype = arrays[0].shape[1:], arrays[0].dtype
    return call(
        functools.partial(join_kernel, plan, held, groups), "join",
        arrays, [VMEM] * len(arrays),
        [((total_size(plan, g), *block), dtype) for g in groups],
    )


class Part:
    def __init__(self, ref, first):
        self.ref, self.first = ref, first

    def __getitem__(self, p):
        return self.ref[self.first + p]


def product_kernel(plan, held, *refs):
    cols, own = refs[:2]
    arrived = {}
    for ref, group in zip(refs[2:2 + len(held)], held):
        for a in group:
            arrived[a] = Part(ref, start_of(plan, group, a))
    away, self_new, total, half = refs[2 + len(held):]
    n = plan.slot_count
    i = plan.row_id(lax.axis_index("row"), lax.axis_index("col"))

    def add_edges(left, scale):
        for a in plan.moved:
            for p, b in enumerate(plan.edges[a]):
                ta, tb = plan.slot[a], plan.slot[b]
                k, j = cols[i * n + ta], cols[i * n + tb]

                @pl.when(cols[k * n + plan.slot[b - a]] == j)
                def _():
                    edge = arrived[a][p + 1]
                    total[tb] += scale * nn(left[ta], edge)
                    total[ta] += scale * nt(left[tb], edge)

    acc = nt(own[0], own[0])
    for s in range(1, n):
        acc = acc + nt(own[s], own[s])
    total[0] = acc
    half[0] = acc.astype(half.dtype)
    for a in plan.moved:
        t = plan.slot[a]
        total[t] = nn(own[0], own[t]) + nn(own[t], arrived[a][0])
    add_edges(own, 1.0)
    for t in range(1, n):
        half[t] = total[t].astype(half.dtype)
    acc = nt(own[0], half[0])
    for s in range(1, n):
        acc = acc + nt(own[s], half[s])
    self_new[0] = 3.0 * total[0] - 2.0 * acc
    t = plan.slot[plan.far]
    cube = nn(own[0], half[t]) + nn(own[t], arrived[plan.far][1])
    self_new[1] = 3.0 * total[t] - 2.0 * cube
    for a in plan.near_moved:
        t = plan.slot[a]
        cube = nn(half[0], own[t]) + nn(half[t], arrived[a][0])
        total[t] = 3.0 * total[t] - 2.0 * cube
    add_edges(half, -2.0)
    for a in plan.near_moved:
        t = plan.slot[a]
        away[t - 1] = total[t].astype(away.dtype)


def home_kernel(plan, *refs):
    cols, (*pieces, p0, q0, p1, q1, r0, r1), outs = refs[0], refs[1:11], refs[11:]
    pieces += [Joined((p0, p1)), Joined((q0, q1)), r0, r1]
    n = plan.slot_count
    my_row, my_col = lax.axis_index("row"), lax.axis_index("col")
    for out, group in zip(outs, home_groups(plan)):
        for p, a in enumerate(group):
            i = plan.row_id(my_row, my_col - a)
            rank = cols[i * n + plan.slot[a]] // plan.grid_cols
            for index, piece in enumerate(pieces):

                @pl.when(rank == piece_rank(plan, my_row, index))
                def _():
                    out[p] = piece[plan.slot[-a] - 1]


def home_groups(plan):
    return [plan.long[e] for e in LONG] + [SHORT] + [[a] for a in plan.alone]


def relay_kernel(plan, *refs):
    longs, near = dict(zip(LONG, refs)), refs[len(LONG)]
    for out, f in zip(refs[len(LONG) + 1:], SHORT):
        out[0] = near[SHORT.index(f)]
        for p, a in enumerate(plan.short[f][1:]):
            e = a - f
            out[p + 1] = longs[e][plan.long[e].index(a)]


def finish_kernel(where, self_new, *refs):
    out = refs[-1]
    out[0, 0] = self_new[0]
    out[0, out.shape[1] - 1] = self_new[1]
    for t, (source, p) in where.items():
        out[0, t] = refs[source][p].astype(jnp.float32).T


VMEM = pl.BlockSpec(memory_space=pltpu.VMEM)
SMEM = pl.BlockSpec(memory_space=pltpu.SMEM)
ANY = pl.BlockSpec(memory_space=pl.ANY)
SMALL = pltpu.CompilerParams(vmem_limit_bytes=12 << 20)


def call(kernel, name, args, specs, outs, scratch=()):
    return pl.pallas_call(
        kernel,
        out_shape=[jax.ShapeDtypeStruct(shape, dtype) for shape, dtype in outs],
        in_specs=specs,
        out_specs=[VMEM] * len(outs),
        scratch_shapes=list(scratch),
        compiler_params=SMALL,
        name=name,
    )(*args)


def per_device(density, cols):
    slot_count, block = density.shape[1], density.shape[2:]
    plan = Plan(slot_count, lax.axis_size("col"), lax.axis_size("row"))
    own, dtype, rows = density[0], density.dtype, plan.grid_rows
    table = cols.reshape(-1)

    def panel_scratch(blocks):
        return [pltpu.VMEM((rows, blocks, *block), dtype), pltpu.SemaphoreType.DMA((rows,))]

    n_kept = len(plan.kept) + 1
    (kept,) = call(
        functools.partial(keep_kernel, plan), "keep", [own], [VMEM], [((n_kept, *block), dtype)]
    )
    groups = pick_groups(plan)
    far, *first, three, minus_three = call(
        functools.partial(pick_kernel, plan), "pick",
        [table, *gather_small(kept)], [SMEM] + [ANY] * rows,
        [((total_size(plan, g), *block), dtype) for g in groups],
        panel_scratch(n_kept),
    )
    far = shifted(far, -plan.far)
    came = {}
    for f, message in zip(FIRST, first):
        if abs(f) == 4:
            message = after(message, far)
        came[f] = shifted(message, -f)
    waiting = {4: (three, [3]), -4: (minus_three, [-3])}
    second, held = [], list(FIRST.values())
    for bundles, sources in THEN:
        arrays, contents = [came[f] for f in sources], [FIRST[f] for f in sources]
        if 4 in sources:
            arrays[0] = after(arrays[0], came[2], came[-2])
        for f in sources:
            if f in waiting:
                arrays.append(waiting[f][0])
                contents.append(waiting[f][1])
        joined = join(plan, arrays, contents, list(bundles.values()))
        second += [shifted(m, -f) for f, m in zip(bundles, joined)]
        held += list(bundles.values())
    came = list(came.values()) + second + [far]
    held.append([plan.far])
    away, self_new = call(
        functools.partial(product_kernel, plan, held), "product",
        [table, own, *came], [SMEM] + [VMEM] * (1 + len(came)),
        [((len(plan.near_moved), *block), dtype), ((2, *block), jnp.float32)],
        [pltpu.VMEM((slot_count, *block), jnp.float32), pltpu.VMEM((slot_count, *block), dtype)],
    )
    groups = home_groups(plan)
    homing = call(
        functools.partial(home_kernel, plan), "home",
        [table, *gather_rows(away)], [SMEM] + [VMEM] * (rows + 2),
        [((len(g), *block), dtype) for g in groups],
    )
    n_long = len(LONG)
    longs = [shifted(m, -e) for m, e in zip(homing, LONG)]
    alone = [shifted(m, -a) for m, a in zip(homing[n_long + 1:], plan.alone)]
    longs = list(lax.optimization_barrier((*longs, *alone)))
    longs, alone = longs[:n_long], longs[n_long:]
    relayed = call(
        functools.partial(relay_kernel, plan), "relay",
        [*longs, homing[n_long]], [VMEM] * (n_long + 1),
        [((len(plan.short[f]), *block), dtype) for f in SHORT],
    )
    shorts = [shifted(m, -f) for m, f in zip(relayed, SHORT)]
    came = longs + alone + shorts
    where = {}
    for source, e in enumerate(LONG):
        if e in plan.long[e]:
            where[plan.slot[e]] = (source, plan.long[e].index(e))
    for source, a in enumerate(plan.alone):
        where[plan.slot[a]] = (n_long + source, 0)
    for source, f in enumerate(SHORT):
        for p, a in enumerate(plan.short[f]):
            where[plan.slot[a]] = (n_long + len(alone) + source, p)
    (new,) = call(
        functools.partial(finish_kernel, where), "finish",
        [self_new, *came], [VMEM] * (1 + len(came)),
        [((1, slot_count, *block), jnp.float32)],
    )
    return new


def solution(mesh):
    in_specs = (P(("row", "col"), None, None, None), P())
    out_specs = P(("row", "col"), None, None, None)
    return jax.shard_map(
        per_device, mesh=mesh, in_specs=in_specs, out_specs=out_specs, check_vma=False
    )
```

```python
import functools

import jax
import jax.numpy as jnp
from jax import lax
from jax.experimental import pallas as pl
from jax.experimental.pallas import tpu as pltpu
from jax.sharding import PartitionSpec as P

SIGNS = {1: 1, 2: 1, 3: -1, 4: 1, 5: -1, 6: -1, 7: 1}
FIRST = {1: [1, 5], -1: [-1, -5], 2: [2, 6], -2: [-2, -6], 4: [4, 7], -4: [-4, -7]}
THEN = [({4: [5], -4: [-5]}, (1, -1)), ({3: [3, 7], -3: [-3, -7]}, (4, -4)), ({4: [6], -4: [-6]}, (2, -2))]
LONG = {4: [4, 5, 3, 6], -4: [-4, -3, -5, -2], 8: [7], -8: [-7, -6]}
SHORT = [1, -1, 2]


class Plan:
    def __init__(self, slot_count, grid_cols, grid_rows):
        half = (slot_count - 2) // 2
        self.slot_count, self.grid_cols, self.grid_rows = slot_count, grid_cols, grid_rows
        self.far = grid_cols // 2
        self.offsets = [0]
        for stride in range(1, half + 1):
            self.offsets += [stride, -stride]
        self.offsets.append(self.far)
        self.slot = {o: s for s, o in enumerate(self.offsets)}
        self.moved = self.offsets[1:]
        near = self.offsets[1:-1]
        self.kept = [0] + [SIGNS.get(d, 1) * d for d in range(1, half + 1)]
        self.place = {d: p for p, d in enumerate(self.kept)}
        self.edges = {self.far: []}
        for a in near:
            self.edges[a] = [b for b in near if b != a and (a - b) in self.place]
        self.size = {a: 1 + len(self.edges[a]) for a in near}
        self.size[self.far] = 2
        self.near_moved = near
        self.long = {e: [a for a in LONG[e] if a in self.slot] for e in LONG}
        relayed = [a for e in LONG for a in self.long[e]]
        self.short = {f: [f] + [a for e in LONG for a in self.long[e] if a - e == f] for f in SHORT}
        self.alone = [a for a in near if a not in relayed and a not in SHORT]

    def row_id(self, rank, col):
        return rank * self.grid_cols + lax.rem(col + 2 * self.grid_cols, self.grid_cols)


def shifted(value, by):
    length = lax.axis_size("col")
    return lax.ppermute(value, "col", [(i, (i + by) % length) for i in range(length)])


def after(value, *others):
    return lax.optimization_barrier((value, *others))[0]


def nn(a, b):
    return lax.dot_general(a, b, (((1,), (0,)), ((), ())), preferred_element_type=jnp.float32)


def nt(a, b):
    return lax.dot_general(a, b, (((1,), (1,)), ((), ())), preferred_element_type=jnp.float32)


def from_chip(block, step):
    length = lax.axis_size("row")
    chips = length // 2
    pairs = [(2 * x + h, 2 * ((x + step) % chips) + h) for x in range(chips) for h in range(2)]
    return lax.ppermute(block, "row", pairs)


def from_core(block):
    return lax.ppermute(block, "row", [(i, i ^ 1) for i in range(lax.axis_size("row"))])


def gather_rows(block):
    half = block.shape[0] // 2
    ahead, behind = from_chip(block, 1), from_chip(block, -1)
    out = []
    for piece in (block, ahead, from_chip(ahead[:half], 1), from_chip(behind[half:], -1), behind):
        out += [piece, from_core(piece)]
    return out


def gather_small(block):
    chips = lax.axis_size("row") // 2
    same = [block] + [None] * (chips - 1)
    same[1], same[chips - 1] = from_chip(block, 1), from_chip(block, chips - 1)
    for step in range(2, chips - 1):
        held, _ = lax.optimization_barrier((block, same[step - 1]))
        same[step] = from_chip(held, step)
    out = []
    for piece in same:
        out += [piece, from_core(piece)]
    return out


def piece_rank(plan, my_row, index):
    chips = plan.grid_rows // 2
    x = lax.rem(my_row // 2 - index // 2 + chips, chips)
    core = lax.rem(my_row, 2)
    if index % 2:
        core = 1 - core
    return 2 * x + core


def land(plan, my_row, pieces, panel, sems):
    copies = []
    for index, piece in enumerate(pieces):
        copy = pltpu.make_async_copy(piece, panel.at[piece_rank(plan, my_row, index)], sems.at[index])
        copy.start()
        copies.append(copy)
    return copies


def keep_kernel(plan, own, out):
    for p, d in enumerate(plan.kept):
        out[p] = own[plan.slot[-d]]
    square = nt(own[0], own[0])
    for s in range(1, plan.slot_count):
        square = square + nt(own[s], own[s])
    out[len(plan.kept)] = square.astype(out.dtype)


class Joined:
    def __init__(self, refs):
        self.first, self.second = refs

    def __getitem__(self, p):
        n = self.first.shape[0]
        return self.first[p] if p < n else self.second[p - n]


def pick_kernel(plan, *refs):
    cols, pieces = refs[0], refs[1:1 + plan.grid_rows]
    outs, (panel, sems) = refs[1 + plan.grid_rows:-2], refs[-2:]
    n = plan.slot_count
    my_row, my_col = lax.axis_index("row"), lax.axis_index("col")
    for copy in land(plan, my_row, pieces, panel, sems):
        copy.wait()
    for out, group in zip(outs, pick_groups(plan)):
        at = 0
        for a in group:
            i = plan.row_id(my_row, my_col - a)
            rank = cols[i * n + plan.slot[a]] // plan.grid_cols
            out[at] = panel[rank, 0]
            if a == plan.far:
                out[at + 1] = panel[rank, len(plan.kept)]
            for p, b in enumerate(plan.edges[a]):
                out[at + p + 1] = panel[rank, plan.place[a - b]]
            at += plan.size[a]


def pick_groups(plan):
    return [[plan.far]] + list(FIRST.values()) + [[3], [-3]]


def total_size(plan, group):
    return sum(plan.size[a] for a in group)


def start_of(plan, group, a):
    return total_size(plan, group[:group.index(a)])


def join_kernel(plan, held, groups, *refs):
    for out, group in zip(refs[len(held):], groups):
        at = 0
        for a in group:
            source = [a in h for h in held].index(True)
            first = start_of(plan, held[source], a)
            for p in range(plan.size[a]):
                out[at + p] = refs[source][first + p]
            at += plan.size[a]


def join(plan, arrays, held, groups):
    block, dtype = arrays[0].shape[1:], arrays[0].dtype
    return call(
        functools.partial(join_kernel, plan, held, groups), "join",
        arrays, [VMEM] * len(arrays),
        [((total_size(plan, g), *block), dtype) for g in groups],
    )


class Part:
    def __init__(self, ref, first):
        self.ref, self.first = ref, first

    def __getitem__(self, p):
        return self.ref[self.first + p]


def parts_of(plan, refs, held):
    arrived = {}
    for ref, group in zip(refs, held):
        for a in group:
            arrived[a] = Part(ref, start_of(plan, group, a))
    return arrived


def add_edges(plan, cols, arrived, strides, left, total, scale):
    n = plan.slot_count
    i = plan.row_id(lax.axis_index("row"), lax.axis_index("col"))
    for a in strides:
        for p, b in enumerate(plan.edges[a]):
            ta, tb = plan.slot[a], plan.slot[b]
            k, j = cols[i * n + ta], cols[i * n + tb]

            @pl.when(cols[k * n + plan.slot[b - a]] == j)
            def _():
                edge = arrived[a][p + 1]
                total[tb] += scale * nn(left[ta], edge)
                total[ta] += scale * nt(left[tb], edge)


def early_kernel(plan, held, *refs):
    cols, own, base = refs[0], refs[1], refs[-1]
    arrived = parts_of(plan, refs[2:-1], held)
    square = nt(own[0], own[0])
    for s in range(1, plan.slot_count):
        square = square + nt(own[s], own[s])
    base[0] = square
    for a in plan.moved:
        t = plan.slot[a]
        base[t] = nn(own[0], own[t])
        if a in FIRST:
            base[t] += nn(own[t], arrived[a][0])
    add_edges(plan, cols, arrived, [a for a in plan.moved if a in FIRST], own, base, 1.0)


def product_kernel(plan, held, *refs):
    cols, own, base = refs[:3]
    arrived = parts_of(plan, refs[3:3 + len(held)], held)
    away, half, far_square, total = refs[3 + len(held):]
    n = plan.slot_count
    for a in plan.moved:
        t = plan.slot[a]
        total[t] = base[t]
        if a not in FIRST:
            total[t] += nn(own[t], arrived[a][0])
    add_edges(plan, cols, arrived, [a for a in plan.moved if a not in FIRST], own, total, 1.0)
    half[0] = base[0].astype(half.dtype)
    for t in range(1, n):
        half[t] = total[t].astype(half.dtype)
    far_square[...] = total[plan.slot[plan.far]]
    for a in plan.near_moved:
        t = plan.slot[a]
        cube = nn(half[0], own[t]) + nn(half[t], arrived[a][0])
        total[t] = 3.0 * total[t] - 2.0 * cube
    add_edges(plan, cols, arrived, plan.moved, half, total, -2.0)
    for a in plan.near_moved:
        t = plan.slot[a]
        away[t - 1] = total[t].astype(away.dtype)


def late_kernel(plan, own, half, base, far_square, far, self_new):
    cube = nt(own[0], half[0])
    for s in range(1, plan.slot_count):
        cube = cube + nt(own[s], half[s])
    self_new[0] = 3.0 * base[0] - 2.0 * cube
    t = plan.slot[plan.far]
    cube = nn(own[0], half[t]) + nn(own[t], far[1])
    self_new[1] = 3.0 * far_square[...] - 2.0 * cube


def home_kernel(plan, *refs):
    cols, (*pieces, p0, q0, p1, q1, r0, r1), outs = refs[0], refs[1:11], refs[11:]
    pieces += [Joined((p0, p1)), Joined((q0, q1)), r0, r1]
    n = plan.slot_count
    my_row, my_col = lax.axis_index("row"), lax.axis_index("col")
    for out, group in zip(outs, home_groups(plan)):
        for p, a in enumerate(group):
            i = plan.row_id(my_row, my_col - a)
            rank = cols[i * n + plan.slot[a]] // plan.grid_cols
            for index, piece in enumerate(pieces):

                @pl.when(rank == piece_rank(plan, my_row, index))
                def _():
                    out[p] = piece[plan.slot[-a] - 1]


def home_groups(plan):
    return [plan.long[e] for e in LONG] + [SHORT] + [[a] for a in plan.alone]


def relay_kernel(plan, *refs):
    longs, near = dict(zip(LONG, refs)), refs[len(LONG)]
    for out, f in zip(refs[len(LONG) + 1:], SHORT):
        out[0] = near[SHORT.index(f)]
        for p, a in enumerate(plan.short[f][1:]):
            e = a - f
            out[p + 1] = longs[e][plan.long[e].index(a)]


def finish_kernel(where, self_new, *refs):
    out = refs[-1]
    out[0, 0] = self_new[0]
    out[0, out.shape[1] - 1] = self_new[1]
    for t, (source, p) in where.items():
        out[0, t] = refs[source][p].astype(jnp.float32).T


VMEM = pl.BlockSpec(memory_space=pltpu.VMEM)
SMEM = pl.BlockSpec(memory_space=pltpu.SMEM)
ANY = pl.BlockSpec(memory_space=pl.ANY)
SMALL = pltpu.CompilerParams(vmem_limit_bytes=12 << 20)


def call(kernel, name, args, specs, outs, scratch=()):
    return pl.pallas_call(
        kernel,
        out_shape=[jax.ShapeDtypeStruct(shape, dtype) for shape, dtype in outs],
        in_specs=specs,
        out_specs=[VMEM] * len(outs),
        scratch_shapes=list(scratch),
        compiler_params=SMALL,
        name=name,
    )(*args)


def per_device(density, cols):
    slot_count, block = density.shape[1], density.shape[2:]
    plan = Plan(slot_count, lax.axis_size("col"), lax.axis_size("row"))
    own, dtype, rows = density[0], density.dtype, plan.grid_rows
    table = cols.reshape(-1)

    def panel_scratch(blocks):
        return [pltpu.VMEM((rows, blocks, *block), dtype), pltpu.SemaphoreType.DMA((rows,))]

    n_kept = len(plan.kept) + 1
    (kept,) = call(
        functools.partial(keep_kernel, plan), "keep", [own], [VMEM], [((n_kept, *block), dtype)]
    )
    groups = pick_groups(plan)
    far, *first, three, minus_three = call(
        functools.partial(pick_kernel, plan), "pick",
        [table, *gather_small(kept)], [SMEM] + [ANY] * rows,
        [((total_size(plan, g), *block), dtype) for g in groups],
        panel_scratch(n_kept),
    )
    far = shifted(far, -plan.far)
    came = {}
    for f, message in zip(FIRST, first):
        if abs(f) == 4:
            message = after(message, far)
        came[f] = shifted(message, -f)
    waiting = {4: (three, [3]), -4: (minus_three, [-3])}
    second, held = [], list(FIRST.values())
    for bundles, sources in THEN:
        arrays, contents = [came[f] for f in sources], [FIRST[f] for f in sources]
        if 4 in sources:
            arrays[0] = after(arrays[0], came[2], came[-2])
        for f in sources:
            if f in waiting:
                arrays.append(waiting[f][0])
                contents.append(waiting[f][1])
        joined = join(plan, arrays, contents, list(bundles.values()))
        second += [shifted(m, -f) for f, m in zip(bundles, joined)]
        held += list(bundles.values())
    came = list(came.values()) + second + [far]
    held.append([plan.far])
    n_first = len(FIRST)
    (base,) = call(
        functools.partial(early_kernel, plan, held[:n_first]), "early",
        [table, own, *came[:n_first]], [SMEM] + [VMEM] * (1 + n_first),
        [((slot_count, *block), jnp.float32)],
    )
    away, half, far_square = call(
        functools.partial(product_kernel, plan, held), "product",
        [table, own, base, *came], [SMEM] + [VMEM] * (2 + len(came)),
        [((len(plan.near_moved), *block), dtype), ((slot_count, *block), dtype), (block, jnp.float32)],
        [pltpu.VMEM((slot_count, *block), jnp.float32)],
    )
    (self_new,) = call(
        functools.partial(late_kernel, plan), "late",
        [own, half, base, far_square, far], [VMEM] * 5, [((2, *block), jnp.float32)],
    )
    groups = home_groups(plan)
    homing = call(
        functools.partial(home_kernel, plan), "home",
        [table, *gather_rows(away)], [SMEM] + [VMEM] * (rows + 2),
        [((len(g), *block), dtype) for g in groups],
    )
    n_long = len(LONG)
    longs = [shifted(m, -e) for m, e in zip(homing, LONG)]
    alone = [shifted(m, -a) for m, a in zip(homing[n_long + 1:], plan.alone)]
    longs = list(lax.optimization_barrier((*longs, *alone)))
    longs, alone = longs[:n_long], longs[n_long:]
    relayed = call(
        functools.partial(relay_kernel, plan), "relay",
        [*longs, homing[n_long]], [VMEM] * (n_long + 1),
        [((len(plan.short[f]), *block), dtype) for f in SHORT],
    )
    shorts = [shifted(m, -f) for m, f in zip(relayed, SHORT)]
    came = longs + alone + shorts
    where = {}
    for source, e in enumerate(LONG):
        if e in plan.long[e]:
            where[plan.slot[e]] = (source, plan.long[e].index(e))
    for source, a in enumerate(plan.alone):
        where[plan.slot[a]] = (n_long + source, 0)
    for source, f in enumerate(SHORT):
        for p, a in enumerate(plan.short[f]):
            where[plan.slot[a]] = (n_long + len(alone) + source, p)
    (new,) = call(
        functools.partial(finish_kernel, where), "finish",
        [self_new, *came], [VMEM] * (1 + len(came)),
        [((1, slot_count, *block), jnp.float32)],
    )
    return new


def solution(mesh):
    in_specs = (P(("row", "col"), None, None, None), P())
    out_specs = P(("row", "col"), None, None, None)
    return jax.shard_map(
        per_device, mesh=mesh, in_specs=in_specs, out_specs=out_specs, check_vma=False
    )
```

```python
import functools

import jax
import jax.numpy as jnp
from jax import lax
from jax.experimental import pallas as pl
from jax.experimental.pallas import tpu as pltpu
from jax.sharding import PartitionSpec as P

SIGNS = {1: 1, 2: 1, 3: -1, 4: 1, 5: -1, 6: -1, 7: 1}
FIRST = {1: [1, 5], -1: [-1, -5], 2: [2, 6], -2: [-2, -6], 4: [4, 7], -4: [-4, -7]}
THEN = [({4: [5], -4: [-5]}, (1, -1)), ({3: [3, 7], -3: [-3, -7]}, (4, -4)), ({4: [6], -4: [-6]}, (2, -2))]
LONG = {4: [4, 5, 3, 6], -4: [-4, -3, -5, -2], 8: [7], -8: [-7, -6]}
SHORT = [2, 1, -1]


class Plan:
    def __init__(self, slot_count, grid_cols, grid_rows):
        half = (slot_count - 2) // 2
        self.slot_count, self.grid_cols, self.grid_rows = slot_count, grid_cols, grid_rows
        self.far = grid_cols // 2
        self.offsets = [0]
        for stride in range(1, half + 1):
            self.offsets += [stride, -stride]
        self.offsets.append(self.far)
        self.slot = {o: s for s, o in enumerate(self.offsets)}
        self.moved = self.offsets[1:]
        near = self.offsets[1:-1]
        self.kept = [0] + [SIGNS.get(d, 1) * d for d in range(1, half + 1)]
        self.place = {d: p for p, d in enumerate(self.kept)}
        self.edges = {self.far: []}
        for a in near:
            self.edges[a] = [b for b in near if b != a and (a - b) in self.place]
        self.size = {a: 1 + len(self.edges[a]) for a in near}
        self.size[self.far] = 2
        self.near_moved = near
        self.long = {e: [a for a in LONG[e] if a in self.slot] for e in LONG}
        relayed = [a for e in LONG for a in self.long[e]]
        self.short = {f: [f] + [a for e in LONG for a in self.long[e] if a - e == f] for f in SHORT}
        self.alone = [a for a in near if a not in relayed and a not in SHORT]

    def row_id(self, rank, col):
        return rank * self.grid_cols + lax.rem(col + 2 * self.grid_cols, self.grid_cols)


def shifted(value, by):
    length = lax.axis_size("col")
    return lax.ppermute(value, "col", [(i, (i + by) % length) for i in range(length)])


def after(value, *others):
    return lax.optimization_barrier((value, *others))[0]


def nn(a, b):
    return lax.dot_general(a, b, (((1,), (0,)), ((), ())), preferred_element_type=jnp.float32)


def nt(a, b):
    return lax.dot_general(a, b, (((1,), (1,)), ((), ())), preferred_element_type=jnp.float32)


def from_chip(block, step):
    length = lax.axis_size("row")
    chips = length // 2
    pairs = [(2 * x + h, 2 * ((x + step) % chips) + h) for x in range(chips) for h in range(2)]
    return lax.ppermute(block, "row", pairs)


def from_core(block):
    return lax.ppermute(block, "row", [(i, i ^ 1) for i in range(lax.axis_size("row"))])


def gather_rows(block):
    half = block.shape[0] // 2
    ahead, behind = from_chip(block, 1), from_chip(block, -1)
    out = []
    for piece in (block, ahead, from_chip(ahead[:half], 1), from_chip(behind[half:], -1), behind):
        out += [piece, from_core(piece)]
    return out


def gather_small(block):
    chips = lax.axis_size("row") // 2
    same = [block] + [None] * (chips - 1)
    same[1], same[chips - 1] = from_chip(block, 1), from_chip(block, chips - 1)
    for step in range(2, chips - 1):
        held, _ = lax.optimization_barrier((block, same[step - 1]))
        same[step] = from_chip(held, step)
    out = []
    for piece in same:
        out += [piece, from_core(piece)]
    return out


def piece_rank(plan, my_row, index):
    chips = plan.grid_rows // 2
    x = lax.rem(my_row // 2 - index // 2 + chips, chips)
    core = lax.rem(my_row, 2)
    if index % 2:
        core = 1 - core
    return 2 * x + core


def land(plan, my_row, pieces, panel, sems):
    copies = []
    for index, piece in enumerate(pieces):
        copy = pltpu.make_async_copy(piece, panel.at[piece_rank(plan, my_row, index)], sems.at[index])
        copy.start()
        copies.append(copy)
    return copies


def keep_kernel(plan, own, out):
    for p, d in enumerate(plan.kept):
        out[p] = own[plan.slot[-d]]
    square = nt(own[0], own[0])
    for s in range(1, plan.slot_count):
        square = square + nt(own[s], own[s])
    out[len(plan.kept)] = square.astype(out.dtype)


class Joined:
    def __init__(self, refs):
        self.first, self.second = refs

    def __getitem__(self, p):
        n = self.first.shape[0]
        return self.first[p] if p < n else self.second[p - n]


def pick_kernel(plan, *refs):
    cols, pieces = refs[0], refs[1:1 + plan.grid_rows]
    outs, (panel, sems) = refs[1 + plan.grid_rows:-2], refs[-2:]
    n = plan.slot_count
    my_row, my_col = lax.axis_index("row"), lax.axis_index("col")
    for copy in land(plan, my_row, pieces, panel, sems):
        copy.wait()
    for out, group in zip(outs, pick_groups(plan)):
        at = 0
        for a in group:
            i = plan.row_id(my_row, my_col - a)
            rank = cols[i * n + plan.slot[a]] // plan.grid_cols
            out[at] = panel[rank, 0]
            if a == plan.far:
                out[at + 1] = panel[rank, len(plan.kept)]
            for p, b in enumerate(plan.edges[a]):
                out[at + p + 1] = panel[rank, plan.place[a - b]]
            at += plan.size[a]


def pick_groups(plan):
    return [[plan.far]] + list(FIRST.values()) + [[3], [-3]]


def total_size(plan, group):
    return sum(plan.size[a] for a in group)


def start_of(plan, group, a):
    return total_size(plan, group[:group.index(a)])


def join_kernel(plan, held, groups, *refs):
    for out, group in zip(refs[len(held):], groups):
        at = 0
        for a in group:
            source = [a in h for h in held].index(True)
            first = start_of(plan, held[source], a)
            for p in range(plan.size[a]):
                out[at + p] = refs[source][first + p]
            at += plan.size[a]


def join(plan, arrays, held, groups):
    block, dtype = arrays[0].shape[1:], arrays[0].dtype
    return call(
        functools.partial(join_kernel, plan, held, groups), "join",
        arrays, [VMEM] * len(arrays),
        [((total_size(plan, g), *block), dtype) for g in groups],
    )


class Part:
    def __init__(self, ref, first):
        self.ref, self.first = ref, first

    def __getitem__(self, p):
        return self.ref[self.first + p]


def parts_of(plan, refs, held):
    arrived = {}
    for ref, group in zip(refs, held):
        for a in group:
            arrived[a] = Part(ref, start_of(plan, group, a))
    return arrived


def add_edges(plan, cols, arrived, strides, left, total, scale):
    n = plan.slot_count
    i = plan.row_id(lax.axis_index("row"), lax.axis_index("col"))
    for a in strides:
        for p, b in enumerate(plan.edges[a]):
            ta, tb = plan.slot[a], plan.slot[b]
            k, j = cols[i * n + ta], cols[i * n + tb]

            @pl.when(cols[k * n + plan.slot[b - a]] == j)
            def _():
                edge = arrived[a][p + 1]
                total[tb] += scale * nn(left[ta], edge)
                total[ta] += scale * nt(left[tb], edge)


def early_kernel(plan, held, *refs):
    cols, own, base = refs[0], refs[1], refs[-1]
    arrived = parts_of(plan, refs[2:-1], held)
    square = nt(own[0], own[0])
    for s in range(1, plan.slot_count):
        square = square + nt(own[s], own[s])
    base[0] = square
    for a in plan.moved:
        t = plan.slot[a]
        base[t] = nn(own[0], own[t])
        if a in FIRST:
            base[t] += nn(own[t], arrived[a][0])
    add_edges(plan, cols, arrived, [a for a in plan.moved if a in FIRST], own, base, 1.0)


def product_kernel(plan, held, *refs):
    cols, own, base = refs[:3]
    arrived = parts_of(plan, refs[3:3 + len(held)], held)
    away, half, far_square, total = refs[3 + len(held):]
    n = plan.slot_count
    for a in plan.moved:
        t = plan.slot[a]
        total[t] = base[t]
        if a not in FIRST:
            total[t] += nn(own[t], arrived[a][0])
    add_edges(plan, cols, arrived, [a for a in plan.moved if a not in FIRST], own, total, 1.0)
    half[0] = base[0].astype(half.dtype)
    for t in range(1, n):
        half[t] = total[t].astype(half.dtype)
    far_square[...] = total[plan.slot[plan.far]]
    for a in plan.near_moved:
        t = plan.slot[a]
        cube = nn(half[0], own[t]) + nn(half[t], arrived[a][0])
        total[t] = 3.0 * total[t] - 2.0 * cube
    add_edges(plan, cols, arrived, plan.moved, half, total, -2.0)
    for a in plan.near_moved:
        t = plan.slot[a]
        away[t - 1] = total[t].astype(away.dtype)


def late_kernel(plan, own, half, base, far_square, far, self_new):
    cube = nt(own[0], half[0])
    for s in range(1, plan.slot_count):
        cube = cube + nt(own[s], half[s])
    self_new[0] = 3.0 * base[0] - 2.0 * cube
    t = plan.slot[plan.far]
    cube = nn(own[0], half[t]) + nn(own[t], far[1])
    self_new[1] = 3.0 * far_square[...] - 2.0 * cube


def home_kernel(plan, *refs):
    cols, (*pieces, p0, q0, p1, q1, r0, r1), outs = refs[0], refs[1:11], refs[11:]
    pieces += [Joined((p0, p1)), Joined((q0, q1)), r0, r1]
    n = plan.slot_count
    my_row, my_col = lax.axis_index("row"), lax.axis_index("col")
    for out, group in zip(outs, home_groups(plan)):
        for p, a in enumerate(group):
            i = plan.row_id(my_row, my_col - a)
            rank = cols[i * n + plan.slot[a]] // plan.grid_cols
            for index, piece in enumerate(pieces):

                @pl.when(rank == piece_rank(plan, my_row, index))
                def _():
                    out[p] = piece[plan.slot[-a] - 1]


def home_groups(plan):
    return [plan.long[e] for e in LONG] + [SHORT] + [[a] for a in plan.alone]


def relay_kernel(plan, *refs):
    longs, near = dict(zip(LONG, refs)), refs[len(LONG)]
    for out, f in zip(refs[len(LONG) + 1:], SHORT):
        out[0] = near[SHORT.index(f)]
        for p, a in enumerate(plan.short[f][1:]):
            e = a - f
            out[p + 1] = longs[e][plan.long[e].index(a)]


def finish_kernel(where, self_new, *refs):
    out = refs[-1]
    out[0, 0] = self_new[0]
    out[0, out.shape[1] - 1] = self_new[1]
    for t, (source, p) in where.items():
        out[0, t] = refs[source][p].astype(jnp.float32).T


VMEM = pl.BlockSpec(memory_space=pltpu.VMEM)
SMEM = pl.BlockSpec(memory_space=pltpu.SMEM)
ANY = pl.BlockSpec(memory_space=pl.ANY)
SMALL = pltpu.CompilerParams(vmem_limit_bytes=12 << 20)


def call(kernel, name, args, specs, outs, scratch=()):
    return pl.pallas_call(
        kernel,
        out_shape=[jax.ShapeDtypeStruct(shape, dtype) for shape, dtype in outs],
        in_specs=specs,
        out_specs=[VMEM] * len(outs),
        scratch_shapes=list(scratch),
        compiler_params=SMALL,
        name=name,
    )(*args)


def per_device(density, cols):
    slot_count, block = density.shape[1], density.shape[2:]
    plan = Plan(slot_count, lax.axis_size("col"), lax.axis_size("row"))
    own, dtype, rows = density[0], density.dtype, plan.grid_rows
    table = cols.reshape(-1)

    def panel_scratch(blocks):
        return [pltpu.VMEM((rows, blocks, *block), dtype), pltpu.SemaphoreType.DMA((rows,))]

    n_kept = len(plan.kept) + 1
    (kept,) = call(
        functools.partial(keep_kernel, plan), "keep", [own], [VMEM], [((n_kept, *block), dtype)]
    )
    groups = pick_groups(plan)
    far, *first, three, minus_three = call(
        functools.partial(pick_kernel, plan), "pick",
        [table, *gather_small(kept)], [SMEM] + [ANY] * rows,
        [((total_size(plan, g), *block), dtype) for g in groups],
        panel_scratch(n_kept),
    )
    far = shifted(far, -plan.far)
    came = {}
    for f, message in zip(FIRST, first):
        if abs(f) == 4:
            message = after(message, far)
        came[f] = shifted(message, -f)
    waiting = {4: (three, [3]), -4: (minus_three, [-3])}
    second, held = [], list(FIRST.values())
    for bundles, sources in THEN:
        arrays, contents = [came[f] for f in sources], [FIRST[f] for f in sources]
        if 4 in sources:
            arrays[0] = after(arrays[0], came[2], came[-2])
        for f in sources:
            if f in waiting:
                arrays.append(waiting[f][0])
                contents.append(waiting[f][1])
        joined = join(plan, arrays, contents, list(bundles.values()))
        second += [shifted(m, -f) for f, m in zip(bundles, joined)]
        held += list(bundles.values())
    came = list(came.values()) + second + [far]
    held.append([plan.far])
    n_first = len(FIRST)
    (base,) = call(
        functools.partial(early_kernel, plan, held[:n_first]), "early",
        [table, own, *came[:n_first]], [SMEM] + [VMEM] * (1 + n_first),
        [((slot_count, *block), jnp.float32)],
    )
    away, half, far_square = call(
        functools.partial(product_kernel, plan, held), "product",
        [table, own, base, *came], [SMEM] + [VMEM] * (2 + len(came)),
        [((len(plan.near_moved), *block), dtype), ((slot_count, *block), dtype), (block, jnp.float32)],
        [pltpu.VMEM((slot_count, *block), jnp.float32)],
    )
    (self_new,) = call(
        functools.partial(late_kernel, plan), "late",
        [own, half, base, far_square, far], [VMEM] * 5, [((2, *block), jnp.float32)],
    )
    groups = home_groups(plan)
    homing = call(
        functools.partial(home_kernel, plan), "home",
        [table, *gather_rows(away)], [SMEM] + [VMEM] * (rows + 2),
        [((len(g), *block), dtype) for g in groups],
    )
    n_long = len(LONG)
    longs = [shifted(m, -e) for m, e in zip(homing, LONG)]
    alone = [shifted(m, -a) for m, a in zip(homing[n_long + 1:], plan.alone)]
    longs = list(lax.optimization_barrier((*longs, *alone)))
    longs, alone = longs[:n_long], longs[n_long:]
    relayed = call(
        functools.partial(relay_kernel, plan), "relay",
        [*longs, homing[n_long]], [VMEM] * (n_long + 1),
        [((len(plan.short[f]), *block), dtype) for f in SHORT],
    )
    shorts = [shifted(m, -f) for m, f in zip(relayed, SHORT)]
    came = longs + alone + shorts
    where = {}
    for source, e in enumerate(LONG):
        if e in plan.long[e]:
            where[plan.slot[e]] = (source, plan.long[e].index(e))
    for source, a in enumerate(plan.alone):
        where[plan.slot[a]] = (n_long + source, 0)
    for source, f in enumerate(SHORT):
        for p, a in enumerate(plan.short[f]):
            where[plan.slot[a]] = (n_long + len(alone) + source, p)
    (new,) = call(
        functools.partial(finish_kernel, where), "finish",
        [self_new, *came], [VMEM] * (1 + len(came)),
        [((1, slot_count, *block), jnp.float32)],
    )
    return new


def solution(mesh):
    in_specs = (P(("row", "col"), None, None, None), P())
    out_specs = P(("row", "col"), None, None, None)
    return jax.shard_map(
        per_device, mesh=mesh, in_specs=in_specs, out_specs=out_specs, check_vma=False
    )
```
